256 devices in a mesh: term: 4 (over x), sector: 64 (over y, z, core).
Axes of the slice: x: 4, y: 4, z: 8, core: 2. Of those that a mesh axis runs over, the one named last changes fastest.
Arguments:
- psi_blocks: bfloat16 [4096, 128, 128], P('sector'), may hold values from -6 to 6
- right_ops: bfloat16 [8, 4096, 128, 128], P('term', 'sector'), may hold values from -0.5 to 0.5
- left_ops: bfloat16 [8, 4096, 128, 128], P('term', 'sector'), may hold values from -0.1875 to 0.1875
- owner_map: int32 [4096, 1], P('sector'), may hold values from 0 to 63; in each aligned block of 64 rows (0 to 63, 64 to 127, ...) at most 2 rows name the same one
- left_local: int32 [4096, 1], P('sector'), may hold values from 0 to 63
Outputs:
- sigma: bfloat16 [4096, 128, 128], P('sector', 'term')
The draws below stay inside these ranges and needn't reach their ends.
Inputs may be any that keep to these rules, and one draw needn't show every extreme that they name: `owner_map`: among the 64 sectors held by one device along `sector` (aligned blocks), at most 2 name the same owner; some block reaches it.
All inputs are finite; a program needn't handle non-finite values.
Results may differ from the reference program's by a relative error of at most 0.0049.
Values may be sent and summed in bfloat16 or wider, within the bound.
A program may use at most 128 MiB of HBM per device.

```python
import math
import jax
import jax.numpy as jnp
import numpy as np
from jax import lax

B = 128
SEC_DEV = 64
SECTORS = 4096
TERMS = 8
CAP = 2
N_SECTOR = 64


def plant(drawn, rng, least, high):
    longest = drawn.shape.index(max(drawn.shape))
    spots = []
    for shift in (0, 1):
        where = [jax.random.randint(jax.random.fold_in(rng, axis), (), 0, length) for axis, length in enumerate(drawn.shape)]
        where[longest] = (where[longest] + shift) % drawn.shape[longest]
        spots.append(tuple(where))
    return drawn.at[spots[0]].set(least).at[spots[1]].set(high)


def block_levels(key, extent, cuts, least, largest):
    level, own = 1.0, jax.random.fold_in(key, 6)
    for position, shards_of in cuts:
        steps = jnp.exp(jax.random.uniform(jax.random.fold_in(own, position), (shards_of,), jnp.float32, least / len(cuts), largest / len(cuts)))
        level = level * jnp.repeat(steps, extent[position] // shards_of).reshape([-1 if axis == position else 1 for axis in range(len(extent))])
    return level


def routed_block(own_key, own, number, rows, amount, top, bound, lean):
    sequence = jax.random.permutation(own_key, amount)
    crowded, usual = load_shares(amount, rows * top, bound, lean, True), load_shares(amount, rows * top, bound, lean, False)
    places = jnp.arange(amount)

    def named(tallies, offset_by):
        used = int((tallies > 0).sum())
        fixed = max(1, used // 4)
        passed = fixed + (places - fixed + offset_by * (used - fixed)) % max(1, amount - fixed)
        return jnp.zeros((amount,), jnp.int32).at[sequence[jnp.where(places < fixed, places, passed)]].set(jnp.asarray(tallies, jnp.int32))

    tallies = jnp.where(number % 4 == 0, named(crowded, number // 4), named(usual, number - number // 4 - 1))
    mixed = jax.random.permutation(jax.random.fold_in(own, 3), amount)
    giver, receiver = mixed[0:amount // 2 * 2:2], mixed[1:amount // 2 * 2:2]
    room = jnp.minimum(tallies[giver] - 1, bound - tallies[receiver]) // 2
    room = jnp.where((giver == sequence[0]) | (receiver == sequence[0]) | (tallies[receiver] == 0), 0, jnp.maximum(room, 0))
    passed = jax.random.randint(jax.random.fold_in(own, 4), (amount // 2,), 0, 1 << 20) % (room + 1)
    tallies = tallies.at[giver].add(-passed).at[receiver].add(passed)
    items = jnp.searchsorted(jnp.cumsum(tallies), jnp.arange(rows * top), side="right").astype(jnp.int32)
    listing = items.reshape(top, rows).T
    listing = listing[jax.random.permutation(jax.random.fold_in(own, 1), rows)]
    offset_by = jax.random.randint(jax.random.fold_in(own, 2), (rows, 1), 0, top)
    return jnp.take_along_axis(listing, (jnp.arange(top)[None, :] + offset_by) % top, axis=1)


def load_shares(amount, total, limit, skew, full):
    portions = [(1 << 20) // math.isqrt(standing ** skew) + 1 for standing in range(1, amount + 1)]
    largest = limit if full else min(limit, max(-(-total // amount), total * portions[0] // sum(portions)))
    least = 1 if total - largest >= amount - 1 else 0
    counts, surplus = [largest] + [least] * (amount - 1), total - largest - least * (amount - 1)
    while surplus > 0:
        candidates = [i for i in range(1, amount) if counts[i] < largest] or [i for i in range(1, amount) if counts[i] < limit]
        mass, budget = sum([portions[i] for i in candidates]), surplus
        for i in candidates:
            addition = min(limit - counts[i], max(1, budget * portions[i] // mass), surplus)
            counts[i] = counts[i] + addition
            surplus = surplus - addition
    return np.array(counts)


def centred(rng, dims, width, limit, pieces=(), held_as=jnp.bfloat16):
    array = width * jax.random.normal(rng, dims, jnp.float32)
    if pieces:
        array = array * block_levels(rng, dims, pieces, -0.22, 0.18)
    return jnp.clip(array, -limit, limit).astype(held_as)


def setup_inputs(seed: int = 0) -> dict:
    key_of = jax.random.split(jax.random.key(seed), 6)
    psi_blocks = centred(key_of[0], (SECTORS, B, B), 1.0, 6.0, ((0, 64),))
    right_ops = centred(key_of[1], (TERMS, SECTORS, B, B), B ** -0.5, 0.5, ((0, 4), (1, 64)))
    left_ops = centred(key_of[2], (TERMS, SECTORS, B, B), (B * TERMS) ** -0.5, 0.1875, ((0, 4), (1, 64)))
    owner_map_keys = jax.random.split(jax.random.fold_in(key_of[3], 1), SECTORS // SEC_DEV)
    owner_map_turns = jax.random.permutation(jax.random.fold_in(key_of[3], 3), SECTORS // SEC_DEV)
    owner_map = jax.vmap(lambda own, number: routed_block(jax.random.fold_in(key_of[3], 2), own, number, SEC_DEV, N_SECTOR, 1, CAP, 2))(owner_map_keys, owner_map_turns).reshape((SECTORS, 1))
    left_local = plant(jax.random.randint(key_of[4], (SECTORS, 1), 0, SEC_DEV), jax.random.fold_in(key_of[4], 1), 0, SEC_DEV - 1).astype(jnp.int32)
    return {"psi_blocks": psi_blocks, "right_ops": right_ops, "left_ops": left_ops, "owner_map": owner_map, "left_local": left_local}


def reference(psi_blocks, right_ops, left_ops, owner_map, left_local):
    target = (owner_map[:, 0] * SEC_DEV + left_local[:, 0]).astype(jnp.int32)
    psi_wide = psi_blocks.astype(jnp.float32)

    def one_term(total, operators):
        right_one, left_one = operators
        inter = jnp.einsum("sij,sjk->sik", psi_wide, right_one.astype(jnp.float32), precision=lax.Precision.HIGHEST).astype(jnp.bfloat16)
        picked = left_one[target].astype(jnp.float32)
        image = jnp.einsum("sij,sjk->sik", picked, inter.astype(jnp.float32), precision=lax.Precision.HIGHEST)
        return total + image, None

    start = jnp.zeros((SECTORS, B, B), jnp.float32)
    total, unused = lax.scan(one_term, start, (right_ops, left_ops))
    sigma = jax.ops.segment_sum(total, target, num_segments=SECTORS)
    return sigma.astype(jnp.bfloat16)
```

```python
import functools

import jax
import jax.numpy as jnp
from jax import lax
from jax.experimental import pallas as pl
from jax.experimental.pallas import tpu as pltpu
from jax.sharding import PartitionSpec as P

CAP = 2


def ranks_of(owners):
    count = owners.shape[-1]
    same = owners[..., :, None] == owners[..., None, :]
    earlier = lax.broadcasted_iota(jnp.int32, (count, count), 0) < lax.broadcasted_iota(
        jnp.int32, (count, count), 1
    )
    return jnp.sum((same & earlier).astype(jnp.int32), axis=-2)


def image_kernel(tags_ref, left_ref, arrived_ref, out_ref, acc):
    slots = arrived_ref.shape[0]
    acc[...] = jnp.zeros_like(acc)

    def step(i, carry):
        tag = tags_ref[i]

        @pl.when(tag >= 0)
        def _():
            lhs = jnp.concatenate([left_ref[0, tag], left_ref[1, tag]], axis=-1)
            acc[tag] += jnp.dot(lhs, arrived_ref[i], preferred_element_type=jnp.float32)

        return carry

    lax.fori_loop(0, slots, step, 0)
    out_ref[...] = acc[...].astype(out_ref.dtype)


def full_exchange(inter, slot_source, left_ops, tags):
    terms, sec_dev, width, _ = left_ops.shape
    packed = jnp.take(inter, slot_source, axis=0, mode="clip")
    arrived = lax.all_to_all(packed, "sector", split_axis=0, concat_axis=0, tiled=True)
    partial = pl.pallas_call(
        image_kernel,
        out_shape=jax.ShapeDtypeStruct((sec_dev, width, width), jnp.bfloat16),
        in_specs=[
            pl.BlockSpec(memory_space=pltpu.SMEM),
            pl.BlockSpec(memory_space=pltpu.VMEM),
            pl.BlockSpec(memory_space=pltpu.VMEM),
        ],
        out_specs=pl.BlockSpec(memory_space=pltpu.VMEM),
        scratch_shapes=[pltpu.VMEM((sec_dev, width, width), jnp.float32)],
        compiler_params=pltpu.CompilerParams(vmem_limit_bytes=48 << 20),
        name="images",
    )(tags, left_ops, arrived)
    total = lax.psum_scatter(
        partial.astype(jnp.float32), "term", scatter_dimension=1, tiled=True
    )
    return total.astype(jnp.bfloat16)


def local(psi_blocks, right_ops, left_ops, owner_map, left_local):
    sec_dev, width, _ = psi_blocks.shape
    terms = right_ops.shape[0]
    n_sector = lax.axis_size("sector")
    slots = n_sector * CAP
    owners = owner_map[:, 0]
    slot_id = owners * CAP + ranks_of(owners)
    hot = slot_id[None, :] == lax.broadcasted_iota(jnp.int32, (slots, sec_dev), 0)
    slot_source = jnp.sum(
        jnp.where(hot, lax.broadcasted_iota(jnp.int32, (slots, sec_dev), 1), 0), axis=1
    )
    routes = lax.all_gather(
        jnp.concatenate([owner_map, left_local], axis=1), "sector", axis=0, tiled=True
    )
    all_owners = routes[:, 0].reshape(n_sector, sec_dev)
    all_local = routes[:, 1].reshape(n_sector, sec_dev)
    mine = lax.axis_index("sector")
    all_ranks = ranks_of(all_owners)
    hits = (all_owners == mine)[:, :, None] & (
        all_ranks[:, :, None] == lax.broadcasted_iota(jnp.int32, (1, 1, CAP), 2)
    )
    tags = (jnp.sum(jnp.where(hits, all_local[:, :, None] + 1, 0), axis=1) - 1).reshape(slots)
    inter = (
        jnp.einsum("sij,tsjk->stik", psi_blocks, right_ops, preferred_element_type=jnp.float32)
        .astype(jnp.bfloat16)
        .reshape(sec_dev, terms * width, width)
    )
    return full_exchange(inter, slot_source, left_ops, tags)


def solution(mesh):
    placed = (
        P("sector", None, None),
        P("term", "sector", None, None),
        P("term", "sector", None, None),
        P("sector", None),
        P("sector", None),
    )
    return jax.shard_map(
        local, mesh=mesh, in_specs=placed, out_specs=P("sector", "term", None), check_vma=False
    )
```

```python
import functools

import jax
import jax.numpy as jnp
from jax import lax
from jax.experimental import pallas as pl
from jax.experimental.pallas import tpu as pltpu
from jax.sharding import PartitionSpec as P

MESH = pl.DeviceIdType.MESH
CAP = 2
NY, NZ, NC = 4, 8, 2
NX = 4
MEMBERS = NY * NC
REACH = (33, 24, 16, 7)
HOPS = len(REACH)


def chunk_bounds(hop):
    edges = [0, *reversed(REACH[hop - 1 :])]
    return list(zip(edges[:-1], edges[1:]))


def ranks_of(owners):
    count = owners.shape[-1]
    same = owners[..., :, None] == owners[..., None, :]
    earlier = lax.broadcasted_iota(jnp.int32, (count, count), 0) < lax.broadcasted_iota(
        jnp.int32, (count, count), 1
    )
    return jnp.sum((same & earlier).astype(jnp.int32), axis=-2)


def plan_of(owners, my_z):
    count = owners.shape[0]
    away = lax.rem(lax.rem(owners // NC, NZ) - my_z + NZ, NZ)
    counts = [jnp.sum((away == d).astype(jnp.int32)) for d in range(NZ)]
    up = [sum(counts[h:HOPS]) for h in range(1, HOPS)] + [0]
    down = [sum(counts[NZ - h] for h in range(k, HOPS)) for k in range(1, HOPS)] + [0]
    room_up = functools.reduce(jnp.minimum, [REACH[h] - up[h] for h in range(HOPS)])
    room_down = functools.reduce(jnp.minimum, [REACH[h] - down[h] for h in range(HOPS)])
    far_up = jnp.clip(room_up, 0, counts[HOPS])
    fits = (room_up >= 0) & (room_down >= counts[HOPS] - far_up)
    opposite = (away == HOPS).astype(jnp.int32)
    row = lax.broadcasted_iota(jnp.int32, (count, count), 0)
    col = lax.broadcasted_iota(jnp.int32, (count, count), 1)
    far_rank = jnp.sum(jnp.where(row < col, opposite[:, None], 0), axis=0)
    signed = jnp.where(
        away == HOPS,
        jnp.where(far_rank < far_up, -HOPS, HOPS),
        jnp.where(away < HOPS, -away, NZ - away),
    )
    key = signed * count + lax.iota(jnp.int32, count)
    position = jnp.sum((key[:, None] < key[None, :]).astype(jnp.int32), axis=0)
    order = jnp.sum(jnp.where(position[None, :] == row, col, 0), axis=1)
    return position, order, fits


def inter_kernel(order, route, psi, right, inter, routes, landing, send_sem, recv_sem):
    n = routes.shape[0]
    count = psi.shape[0]
    width = psi.shape[1]
    me = lax.axis_index("sector")
    barrier = pltpu.get_barrier_semaphore()

    def greet(o, carry):
        pl.semaphore_signal(
            barrier, inc=1, device_id={"sector": (me + o) % n}, device_id_type=MESH
        )
        return carry

    lax.fori_loop(1, n, greet, 0)

    def multiply(p, carry):
        s = order[p]
        both = jnp.concatenate([right[0, s], right[1, s]], axis=-1)
        made = jnp.dot(psi[s], both, preferred_element_type=jnp.float32).astype(inter.dtype)
        inter[p, :width] = made[:, :width]
        inter[p, width:] = made[:, width:]
        return carry

    lax.fori_loop(0, count // 2, multiply, 0, unroll=4)
    pl.semaphore_wait(barrier, n - 1)

    def copy_of(o):
        return pltpu.make_async_remote_copy(
            src_ref=route,
            dst_ref=landing.at[me],
            send_sem=send_sem.at[o],
            recv_sem=recv_sem.at[o],
            device_id={"sector": (me + o) % n},
            device_id_type=MESH,
        )

    def send(o, carry):
        copy_of(o).start()
        return carry

    lax.fori_loop(1, n, send, 0)
    lax.fori_loop(count // 2, count, multiply, 0, unroll=4)

    def finish(o, carry):
        copy_of(o).wait_send()
        copy_of(o).wait_recv()
        return carry

    lax.fori_loop(1, n, finish, 0)
    landing[me] = route[...]
    routes[...] = landing[...]


def ring_kernel(
    pick, tags, inter, left, out,
    up1, up2, up3, down1, down2, down3, far, outgoing, arrived, shares, taken,
    ring_send, ring_recv, row_send, row_recv, term_send, term_recv,
):
    count = inter.shape[0]
    width = inter.shape[2]
    tall = inter.shape[1]
    rows = out.shape[1]
    per_source = MEMBERS * CAP
    x = lax.axis_index("term")
    place = lax.axis_index("sector")
    c = place % NC
    z = (place // NC) % NZ
    y = place // (NC * NZ)
    my_member = y * NC + c

    def sector_id(yy, zz, cc):
        return {"sector": (yy * NZ + zz) * NC + cc}

    def member_of(j):
        return (y + j // NC) % NY, (c + j) % NC

    z_up, z_down = (z + 1) % NZ, (z + NZ - 1) % NZ
    barrier = pltpu.get_barrier_semaphore()
    pl.semaphore_signal(barrier, inc=1, device_id=sector_id(y, z_up, c), device_id_type=MESH)
    pl.semaphore_signal(barrier, inc=1, device_id=sector_id(y, z_down, c), device_id_type=MESH)
    for j in range(1, MEMBERS):
        yy, cc = member_of(j)
        pl.semaphore_signal(barrier, inc=1, device_id=sector_id(yy, z, cc), device_id_type=MESH)
    for d in range(1, NX):
        pl.semaphore_signal(barrier, inc=1, device_id={"term": (x + d) % NX}, device_id_type=MESH)
    pl.semaphore_wait(barrier, 2 + MEMBERS - 1 + NX - 1)

    reach_far = REACH[-1]
    up = (inter, up1, up2, up3, far)
    down = (inter, down1, down2, down3, far)
    number = {}
    for hop in range(1, HOPS + 1):
        for k in range(len(chunk_bounds(hop))):
            number[hop, k] = len(number)

    def ring_copy(way, hop, k):
        near, end = chunk_bounds(hop)[k]
        size = end - near
        if way == 0:
            source, target, neighbour = up[hop - 1], up[hop], z_up
            src_at, dst_at = near, near
        else:
            source, target, neighbour = down[hop - 1], down[hop], z_down
            held = count if hop == 1 else REACH[hop - 2]
            src_at = held - end
            dst_at = REACH[hop - 1] - end + (reach_far if hop == HOPS else 0)
        return pltpu.make_async_remote_copy(
            src_ref=source.at[pl.ds(src_at, size)],
            dst_ref=target.at[pl.ds(dst_at, size)],
            send_sem=ring_send.at[way, number[hop, k]],
            recv_sem=ring_recv.at[way, number[hop, k]],
            device_id=sector_id(y, neighbour, c),
            device_id_type=MESH,
        )

    def row_copy(d, j):
        yy, cc = member_of(j)
        return pltpu.make_async_remote_copy(
            src_ref=outgoing.at[d, j],
            dst_ref=arrived.at[(z + NZ - d) % NZ, my_member],
            send_sem=row_send.at[d, j],
            recv_sem=row_recv.at[d, j],
            device_id=sector_id(yy, z, cc),
            device_id_type=MESH,
        )

    def term_copy(d, dx):
        group = pl.ds(((z + NZ - d) % NZ) * per_source, per_source)
        return pltpu.make_async_remote_copy(
            src_ref=shares.at[dx - 1, group],
            dst_ref=taken.at[dx - 1, group],
            send_sem=term_send.at[d, dx],
            recv_sem=term_recv.at[d, dx],
            device_id={"term": (x + dx) % NX},
            device_id_type=MESH,
        )

    def hand_on(d, held):
        source = (z + NZ - d) % NZ

        def one(j, carry):
            yy, cc = member_of(j)
            entry = (source * MEMBERS + yy * NC + cc) * CAP
            outgoing[d, j, :tall] = held[pick[entry]]
            outgoing[d, j, tall:] = held[pick[entry + 1]]
            row_copy(d, j).start()
            return carry

        lax.fori_loop(1, MEMBERS, one, 0)
        entry = (source * MEMBERS + my_member) * CAP
        arrived[source, my_member, :tall] = held[pick[entry]]
        arrived[source, my_member, tall:] = held[pick[entry + 1]]

    def images(d):
        source = (z + NZ - d) % NZ

        def landed(j, carry):
            row_copy(d, j).wait_recv()
            return carry

        lax.fori_loop(1, MEMBERS, landed, 0)

        def one(m, carry):
            for r in range(CAP):
                slot = source * per_source + m * CAP + r
                tag = tags[slot]
                lhs = jnp.concatenate(
                    [
                        jnp.concatenate(
                            [left[t, tag, pl.ds(((x + dx) % NX) * rows, rows)] for dx in range(NX)],
                            axis=0,
                        )
                        for t in range(2)
                    ],
                    axis=1,
                )
                image = jnp.dot(
                    lhs,
                    arrived[source, m, r * tall : (r + 1) * tall],
                    preferred_element_type=jnp.float32,
                )
                out[slot] = image[:rows]
                for dx in range(1, NX):
                    shares[dx - 1, slot] = image[dx * rows : (dx + 1) * rows].astype(shares.dtype)
            return carry

        lax.fori_loop(0, MEMBERS, one, 0)
        for dx in range(1, NX):
            term_copy(d, dx).start()

    for k in range(len(chunk_bounds(1))):
        ring_copy(0, 1, k).start()
        ring_copy(1, 1, k).start()
    hand_on(0, inter)
    waiting = [0]
    for hop in range(1, HOPS + 1):
        pieces = len(chunk_bounds(hop))
        for k in range(pieces):
            for way in range(2):
                ring_copy(way, hop, k).wait_recv()
                if k < pieces - 1:
                    ring_copy(way, hop + 1, k).start()
        if hop < HOPS:
            hand_on(hop, up[hop])
            hand_on(NZ - hop, down[hop])
            arriving = [hop, NZ - hop]
        else:
            hand_on(hop, far)
            arriving = [hop]
        for d in waiting:
            images(d)
        waiting = arriving
    for d in waiting:
        images(d)

    def settle(d, carry):
        for dx in range(1, NX):
            term_copy(d, dx).wait_recv()
        return carry

    lax.fori_loop(0, NZ, settle, 0)

    def total(slot, carry):
        out[slot] = out[slot] + (
            taken[0, slot].astype(jnp.float32)
            + taken[1, slot].astype(jnp.float32)
            + taken[2, slot].astype(jnp.float32)
        )
        return carry

    lax.fori_loop(0, out.shape[0], total, 0, unroll=4)

    for way in range(2):
        for hop, k in number:
            ring_copy(way, hop, k).wait_send()

    def sent(d, carry):
        for j in range(1, MEMBERS):
            row_copy(d, j).wait_send()
        for dx in range(1, NX):
            term_copy(d, dx).wait_send()
        return carry

    lax.fori_loop(0, NZ, sent, 0)


def gather_kernel(tags, found, out, acc):
    acc[...] = jnp.zeros_like(acc)

    def step(i, carry):
        tag = tags[i]

        @pl.when(tag >= 0)
        def _():
            acc[tag] += found[i]

        return carry

    lax.fori_loop(0, found.shape[0], step, 0)
    out[...] = acc[...].astype(out.dtype)


def image_kernel(tags_ref, left_ref, arrived_ref, out_ref, acc):
    slots = arrived_ref.shape[0]
    acc[...] = jnp.zeros_like(acc)

    def step(i, carry):
        tag = tags_ref[i]

        @pl.when(tag >= 0)
        def _():
            lhs = jnp.concatenate([left_ref[0, tag], left_ref[1, tag]], axis=-1)
            acc[tag] += jnp.dot(lhs, arrived_ref[i], preferred_element_type=jnp.float32)

        return carry

    lax.fori_loop(0, slots, step, 0)
    out_ref[...] = acc[...].astype(out_ref.dtype)


def full_exchange(inter, slot_source, left_ops, tags):
    terms, sec_dev, width, _ = left_ops.shape
    packed = jnp.take(inter, slot_source, axis=0, mode="clip")
    arrived = lax.all_to_all(packed, "sector", split_axis=0, concat_axis=0, tiled=True)
    partial = pl.pallas_call(
        image_kernel,
        out_shape=jax.ShapeDtypeStruct((sec_dev, width, width), jnp.float32),
        in_specs=[
            pl.BlockSpec(memory_space=pltpu.SMEM),
            pl.BlockSpec(memory_space=pltpu.VMEM),
            pl.BlockSpec(memory_space=pltpu.VMEM),
        ],
        out_specs=pl.BlockSpec(memory_space=pltpu.VMEM),
        scratch_shapes=[pltpu.VMEM((sec_dev, width, width), jnp.float32)],
        compiler_params=pltpu.CompilerParams(vmem_limit_bytes=48 << 20),
        name="images",
    )(tags, left_ops, arrived)
    total = lax.psum_scatter(partial, "term", scatter_dimension=1, tiled=True)
    return total.astype(jnp.bfloat16)


def ring_exchange(inter, pick, tags, left_ops):
    terms, sec_dev, width, _ = left_ops.shape
    tall = inter.shape[1]
    slots = tags.shape[0]
    rows = width // NX
    smem = pl.BlockSpec(memory_space=pltpu.SMEM)
    vmem = pl.BlockSpec(memory_space=pltpu.VMEM)
    dma = pltpu.SemaphoreType.DMA
    pieces = sum(range(1, HOPS + 1))
    found = pl.pallas_call(
        ring_kernel,
        out_shape=jax.ShapeDtypeStruct((slots, rows, width), jnp.float32),
        in_specs=[smem, smem, vmem, vmem],
        out_specs=vmem,
        scratch_shapes=[
            pltpu.VMEM((REACH[0], tall, width), jnp.bfloat16),
            pltpu.VMEM((REACH[1], tall, width), jnp.bfloat16),
            pltpu.VMEM((REACH[2], tall, width), jnp.bfloat16),
            pltpu.VMEM((REACH[0], tall, width), jnp.bfloat16),
            pltpu.VMEM((REACH[1], tall, width), jnp.bfloat16),
            pltpu.VMEM((REACH[2], tall, width), jnp.bfloat16),
            pltpu.VMEM((2 * REACH[3], tall, width), jnp.bfloat16),
            pltpu.VMEM((NZ, MEMBERS, CAP * tall, width), jnp.bfloat16),
            pltpu.VMEM((NZ, MEMBERS, CAP * tall, width), jnp.bfloat16),
            pltpu.VMEM((NX - 1, slots, rows, width), jnp.bfloat16),
            pltpu.VMEM((NX - 1, slots, rows, width), jnp.bfloat16),
            dma((2, pieces)),
            dma((2, pieces)),
            dma((NZ, MEMBERS)),
            dma((NZ, MEMBERS)),
            dma((NZ, NX)),
            dma((NZ, NX)),
        ],
        compiler_params=pltpu.CompilerParams(
            collective_id=1, has_side_effects=True, vmem_limit_bytes=62 << 20
        ),
        name="ring",
    )(pick, jnp.maximum(tags, 0), inter, left_ops)
    return pl.pallas_call(
        gather_kernel,
        out_shape=jax.ShapeDtypeStruct((sec_dev, rows, width), jnp.bfloat16),
        in_specs=[smem, vmem],
        out_specs=vmem,
        scratch_shapes=[pltpu.VMEM((sec_dev, rows, width), jnp.float32)],
        name="gather",
    )(tags, found)


def local(psi_blocks, right_ops, left_ops, owner_map, left_local):
    sec_dev, width, _ = psi_blocks.shape
    terms = right_ops.shape[0]
    n_sector = lax.axis_size("sector")
    slots = n_sector * CAP
    mine = lax.axis_index("sector")
    my_c, my_z, my_y = mine % NC, (mine // NC) % NZ, mine // (NC * NZ)
    owners = owner_map[:, 0]
    ranks = ranks_of(owners)
    position, order, fits = plan_of(owners, my_z)
    route = jnp.concatenate(
        [owners, left_local[:, 0], jnp.where(fits, position, -1), ranks]
    ).reshape(2, 2 * sec_dev)

    smem = pl.BlockSpec(memory_space=pltpu.SMEM)
    vmem = pl.BlockSpec(memory_space=pltpu.VMEM)
    inter, routes = pl.pallas_call(
        inter_kernel,
        out_shape=(
            jax.ShapeDtypeStruct((sec_dev, terms * width, width), jnp.bfloat16),
            jax.ShapeDtypeStruct((n_sector, 2, 2 * sec_dev), jnp.int32),
        ),
        in_specs=[smem, vmem, vmem, vmem],
        out_specs=(vmem, vmem),
        scratch_shapes=[
            pltpu.VMEM((n_sector, 2, 2 * sec_dev), jnp.int32),
            pltpu.SemaphoreType.DMA((n_sector,)),
            pltpu.SemaphoreType.DMA((n_sector,)),
        ],
        compiler_params=pltpu.CompilerParams(
            collective_id=0, has_side_effects=True, vmem_limit_bytes=48 << 20
        ),
        name="inter",
    )(order, route, psi_blocks, right_ops)

    routes = routes.reshape(n_sector, 4, sec_dev)
    all_owners, all_local, all_positions, all_ranks = (routes[:, k] for k in range(4))
    all_fit = jnp.min(all_positions) >= 0

    hits = (all_owners == mine)[:, None, :] & (
        all_ranks[:, None, :] == lax.broadcasted_iota(jnp.int32, (1, CAP, 1), 1)
    )
    tags = jnp.sum(jnp.where(hits, all_local[:, None, :] + 1, 0), axis=2) - 1

    ring = lax.dynamic_index_in_dim(
        lax.dynamic_index_in_dim(
            routes.reshape(NY, NZ, NC, 4, sec_dev), my_y, axis=0, keepdims=False
        ),
        my_c,
        axis=1,
        keepdims=False,
    )
    member = lax.broadcasted_iota(jnp.int32, (1, MEMBERS, 1, 1), 1)
    goal = ((member // NC) * NZ + my_z) * NC + member % NC
    for_member = (ring[:, None, None, 0] == goal) & (
        ring[:, None, None, 3] == lax.broadcasted_iota(jnp.int32, (1, 1, CAP, 1), 2)
    )
    back = lax.rem(my_z - lax.iota(jnp.int32, NZ) + NZ, NZ)
    start = jnp.zeros_like(back)
    for h in range(1, HOPS):
        start = jnp.where(back == NZ - h, sec_dev - REACH[h - 1], start)
    place = ring[:, 2] - start[:, None]
    place = jnp.where(
        (back[:, None] == HOPS) & (place >= REACH[-1]), place - (sec_dev - 2 * REACH[-1]), place
    )
    pick = jnp.sum(jnp.where(for_member, place[:, None, None, :], 0), axis=3).reshape(slots)

    def by_ring(inter, left_ops):
        spread = tags.reshape(NY, NZ, NC, CAP).transpose(1, 0, 2, 3).reshape(slots)
        return ring_exchange(inter, pick, spread, left_ops)

    def by_all(inter, left_ops):
        slot_id = owners * CAP + ranks
        hot = slot_id[None, :] == lax.broadcasted_iota(jnp.int32, (slots, sec_dev), 0)
        slot_source = jnp.sum(jnp.where(hot, position[None, :], 0), axis=1)
        return full_exchange(inter, slot_source, left_ops, tags.reshape(slots))

    return lax.cond(all_fit, by_ring, by_all, inter, left_ops)


def solution(mesh):
    placed = (
        P("sector", None, None),
        P("term", "sector", None, None),
        P("term", "sector", None, None),
        P("sector", None),
        P("sector", None),
    )
    return jax.shard_map(
        local, mesh=mesh, in_specs=placed, out_specs=P("sector", "term", None), check_vma=False
    )
```

```python
import functools

import jax
import jax.numpy as jnp
from jax import lax
from jax.experimental import pallas as pl
from jax.experimental.pallas import tpu as pltpu
from jax.sharding import PartitionSpec as P

MESH = pl.DeviceIdType.MESH
CAP = 2
NY, NZ, NC = 4, 8, 2
NX = 4
MEMBERS = NY * NC
REACH = (33, 24, 16, 7)
HOPS = len(REACH)


def chunk_bounds(hop):
    edges = [0, *reversed(REACH[hop - 1 :])]
    return list(zip(edges[:-1], edges[1:]))


def ranks_of(owners):
    count = owners.shape[-1]
    same = owners[..., :, None] == owners[..., None, :]
    earlier = lax.broadcasted_iota(jnp.int32, (count, count), 0) < lax.broadcasted_iota(
        jnp.int32, (count, count), 1
    )
    return jnp.sum((same & earlier).astype(jnp.int32), axis=-2)


def plan_of(owners, my_z):
    count = owners.shape[0]
    away = lax.rem(lax.rem(owners // NC, NZ) - my_z + NZ, NZ)
    counts = [jnp.sum((away == d).astype(jnp.int32)) for d in range(NZ)]
    up = [sum(counts[h:HOPS]) for h in range(1, HOPS)] + [0]
    down = [sum(counts[NZ - h] for h in range(k, HOPS)) for k in range(1, HOPS)] + [0]
    room_up = functools.reduce(jnp.minimum, [REACH[h] - up[h] for h in range(HOPS)])
    room_down = functools.reduce(jnp.minimum, [REACH[h] - down[h] for h in range(HOPS)])
    far_up = jnp.clip(room_up, 0, counts[HOPS])
    fits = (room_up >= 0) & (room_down >= counts[HOPS] - far_up)
    opposite = (away == HOPS).astype(jnp.int32)
    row = lax.broadcasted_iota(jnp.int32, (count, count), 0)
    col = lax.broadcasted_iota(jnp.int32, (count, count), 1)
    far_rank = jnp.sum(jnp.where(row < col, opposite[:, None], 0), axis=0)
    signed = jnp.where(
        away == HOPS,
        jnp.where(far_rank < far_up, -HOPS, HOPS),
        jnp.where(away < HOPS, -away, NZ - away),
    )
    key = signed * count + lax.iota(jnp.int32, count)
    position = jnp.sum((key[:, None] < key[None, :]).astype(jnp.int32), axis=0)
    order = jnp.sum(jnp.where(position[None, :] == row, col, 0), axis=1)
    return position, order, fits


def tables_of(owners, ranks, left_local, position, fits, my_z):
    count = owners.shape[0]
    shape = (NZ, MEMBERS * CAP, count)
    mate = lax.broadcasted_iota(jnp.int32, shape, 0)
    member = lax.broadcasted_iota(jnp.int32, shape, 1) // CAP
    rank = lax.broadcasted_iota(jnp.int32, shape, 1) % CAP
    goal = ((member // NC) * NZ + mate) * NC + member % NC
    hits = (owners == goal) & (ranks == rank)
    ahead = lax.rem(lax.iota(jnp.int32, NZ) - my_z + NZ, NZ)[:, None]
    start, size = jnp.zeros_like(ahead), jnp.full_like(ahead, count)
    for h in range(1, HOPS):
        start = jnp.where(ahead == NZ - h, count - REACH[h - 1], start)
        size = jnp.where((ahead == h) | (ahead == NZ - h), REACH[h - 1], size)
    size = jnp.where(ahead == HOPS, 2 * REACH[-1], size)
    where = jnp.sum(jnp.where(hits, position, 0), axis=2) - start
    where = jnp.where(
        (ahead == HOPS) & (where >= REACH[-1]), where - (count - 2 * REACH[-1]), where
    )
    where = jnp.clip(where, 0, size - 1)
    tags = jnp.sum(jnp.where(hits, left_local + 1, 0), axis=2) - 1
    flag = jnp.broadcast_to(fits.astype(jnp.int32), (NZ, 128 - 2 * MEMBERS * CAP))
    return jnp.concatenate([where, tags, flag], axis=1).reshape(NZ, 1, 128)


def ring_kernel(
    order, table, psi_far, right_far, left_far, out, all_tables,
    psi, right, left, inter0, inter1,
    up10, up20, up30, down10, down20, down30, far0,
    up11, up21, up31, down11, down21, down31, far1,
    outgoing, arrived, shares, taken, mates, picks, rowmates, tags,
    load, local_sem, ring_send, ring_recv, row_send, row_recv, term_send, term_recv,
    mate_send, mate_recv, table_send, table_recv,
):
    count, width = psi.shape[0], psi.shape[1]
    rows = out.shape[1]
    per_source = MEMBERS * CAP
    x = lax.axis_index("term")
    place = lax.axis_index("sector")
    c = place % NC
    z = (place // NC) % NZ
    y = place // (NC * NZ)
    my_member = y * NC + c

    def sector_id(yy, zz, cc):
        return {"sector": (yy * NZ + zz) * NC + cc}

    def member_of(j):
        return (y + j // NC) % NY, (c + j) % NC

    z_up, z_down = (z + 1) % NZ, (z + NZ - 1) % NZ
    loads = [
        pltpu.make_async_copy(psi_far, psi, load.at[0]),
        pltpu.make_async_copy(right_far, right, load.at[1]),
        pltpu.make_async_copy(left_far, left, load.at[2]),
    ]
    for copy in loads:
        copy.start()
    own_row = pltpu.make_async_copy(table.at[z], mates.at[z], local_sem.at[0])
    own_row.start()
    barrier = pltpu.get_barrier_semaphore()
    for d in range(1, NZ):
        pl.semaphore_signal(
            barrier, inc=1, device_id=sector_id(y, (z + d) % NZ, c), device_id_type=MESH
        )
    for j in range(1, MEMBERS):
        yy, cc = member_of(j)
        pl.semaphore_signal(barrier, inc=1, device_id=sector_id(yy, z, cc), device_id_type=MESH)
    for d in range(1, NX):
        pl.semaphore_signal(barrier, inc=1, device_id={"term": (x + d) % NX}, device_id_type=MESH)

    inter = (inter0, inter1)
    up = ((inter0, up10, up20, up30, far0), (inter1, up11, up21, up31, far1))
    down = ((inter0, down10, down20, down30, far0), (inter1, down11, down21, down31, far1))
    reach_far = REACH[-1]
    number = {}
    for hop in range(1, HOPS + 1):
        for k in range(len(chunk_bounds(hop))):
            number[hop, k] = len(number)

    def ring_copy(w, way, hop, k):
        near, end = chunk_bounds(hop)[k]
        size = end - near
        if way == 0:
            source, target, neighbour = up[w][hop - 1], up[w][hop], z_up
            src_at, dst_at = near, near
        else:
            source, target, neighbour = down[w][hop - 1], down[w][hop], z_down
            held = count if hop == 1 else REACH[hop - 2]
            src_at = held - end
            dst_at = REACH[hop - 1] - end + (reach_far if hop == HOPS else 0)
        return pltpu.make_async_remote_copy(
            src_ref=source.at[pl.ds(src_at, size)],
            dst_ref=target.at[pl.ds(dst_at, size)],
            send_sem=ring_send.at[w, way, number[hop, k]],
            recv_sem=ring_recv.at[w, way, number[hop, k]],
            device_id=sector_id(y, neighbour, c),
            device_id_type=MESH,
        )

    def row_copy(w, d, j):
        yy, cc = member_of(j)
        return pltpu.make_async_remote_copy(
            src_ref=outgoing.at[w, d, j],
            dst_ref=arrived.at[w, (z + NZ - d) % NZ, my_member],
            send_sem=row_send.at[w, d, j],
            recv_sem=row_recv.at[w, d, j],
            device_id=sector_id(yy, z, cc),
            device_id_type=MESH,
        )

    def term_copy(d, dx):
        group = pl.ds(((z + NZ - d) % NZ) * per_source, per_source)
        return pltpu.make_async_remote_copy(
            src_ref=shares.at[dx - 1, group],
            dst_ref=taken.at[dx - 1, group],
            send_sem=term_send.at[d, dx],
            recv_sem=term_recv.at[d, dx],
            device_id={"term": (x + dx) % NX},
            device_id_type=MESH,
        )

    def mate_copy(d):
        mate = (z + d) % NZ
        return pltpu.make_async_remote_copy(
            src_ref=table.at[mate],
            dst_ref=mates.at[z],
            send_sem=mate_send.at[d],
            recv_sem=mate_recv.at[d],
            device_id=sector_id(y, mate, c),
            device_id_type=MESH,
        )

    def table_copy(j):
        yy, cc = member_of(j)
        return pltpu.make_async_remote_copy(
            src_ref=mates,
            dst_ref=rowmates.at[my_member],
            send_sem=table_send.at[j],
            recv_sem=table_recv.at[j],
            device_id=sector_id(yy, z, cc),
            device_id_type=MESH,
        )

    def multiply(p, carry):
        s = order[p]
        both = jnp.concatenate([right[0, s], right[1, s]], axis=-1)
        made = jnp.dot(psi[s], both, preferred_element_type=jnp.float32).astype(inter0.dtype)
        inter0[p] = made[:, :width]
        inter1[p] = made[:, width:]
        return carry

    def hand_on(w, d, held):
        source = (z + NZ - d) % NZ

        def one(j, carry):
            yy, cc = member_of(j)
            entry = (yy * NC + cc) * CAP
            outgoing[w, d, j, :width] = held[picks[source, 0, entry]]
            outgoing[w, d, j, width:] = held[picks[source, 0, entry + 1]]
            row_copy(w, d, j).start()
            return carry

        lax.fori_loop(1, MEMBERS, one, 0)
        entry = my_member * CAP
        arrived[w, source, my_member, :width] = held[picks[source, 0, entry]]
        arrived[w, source, my_member, width:] = held[picks[source, 0, entry + 1]]

    def images(d):
        source = (z + NZ - d) % NZ

        def landed(j, carry):
            row_copy(0, d, j).wait_recv()
            row_copy(1, d, j).wait_recv()
            return carry

        lax.fori_loop(1, MEMBERS, landed, 0)

        def one(m, carry):
            for r in range(CAP):
                slot = source * per_source + m * CAP + r
                tag = jnp.maximum(tags[m, source, 0, per_source + my_member * CAP + r], 0)
                lhs = jnp.concatenate(
                    [
                        jnp.concatenate(
                            [left[t, tag, pl.ds(((x + dx) % NX) * rows, rows)] for dx in range(NX)],
                            axis=0,
                        )
                        for t in range(2)
                    ],
                    axis=1,
                )
                rhs = jnp.concatenate(
                    [arrived[t, source, m, r * width : (r + 1) * width] for t in range(2)], axis=0
                )
                image = jnp.dot(lhs, rhs, preferred_element_type=jnp.float32)
                out[slot] = image[:rows]
                for dx in range(1, NX):
                    shares[dx - 1, slot] = image[dx * rows : (dx + 1) * rows].astype(shares.dtype)
            return carry

        lax.fori_loop(0, MEMBERS, one, 0)
        for dx in range(1, NX):
            term_copy(d, dx).start()

    loads[0].wait()
    loads[1].wait()
    edges = [0, *reversed(REACH)]
    spans = [
        [(edges[k], edges[k + 1]), (count - edges[k + 1], count - edges[k])] for k in range(HOPS)
    ]
    spans[-1] = [(edges[HOPS - 1], count - edges[HOPS - 1])]
    for k in range(HOPS):
        for low, high in spans[k]:
            lax.fori_loop(low, high, multiply, 0, unroll=True)
        if k == 0:
            pl.semaphore_wait(barrier, NZ - 1 + MEMBERS - 1 + NX - 1)
            for d in range(1, NZ):
                mate_copy(d).start()
        ring_copy(0, 0, 1, k).start()
        ring_copy(0, 1, 1, k).start()

    own_row.wait()
    for d in range(1, NZ):
        mate_copy(d).wait_recv()
    for j in range(1, MEMBERS):
        table_copy(j).start()
    to_picks = pltpu.make_async_copy(mates, picks, local_sem.at[1])
    to_picks.start()
    own_rows = pltpu.make_async_copy(mates, rowmates.at[my_member], local_sem.at[2])
    own_rows.start()
    to_picks.wait()
    for w in range(2):
        hand_on(w, 0, inter[w])
    own_rows.wait()
    for j in range(1, MEMBERS):
        table_copy(j).wait_recv()
    to_tags = pltpu.make_async_copy(rowmates, tags, local_sem.at[3])
    to_tags.start()
    to_tags.wait()
    for m in range(MEMBERS):
        all_tables[m] = rowmates[m]
    loads[2].wait()

    waiting = [0]
    for w in range(2):
        for hop in range(1, HOPS + 1):
            pieces = len(chunk_bounds(hop))
            for k in range(pieces):
                for way in range(2):
                    ring_copy(w, way, hop, k).wait_recv()
                if k < pieces - 1:
                    between = w == 0 and hop == HOPS - 1
                    if between:
                        for late in range(HOPS - 1):
                            ring_copy(1, 0, 1, late).start()
                            ring_copy(1, 1, 1, late).start()
                    ring_copy(w, 0, hop + 1, k).start()
                    ring_copy(w, 1, hop + 1, k).start()
                    if between:
                        ring_copy(1, 0, 1, HOPS - 1).start()
                        ring_copy(1, 1, 1, HOPS - 1).start()
            if hop < HOPS:
                hand_on(w, hop, up[w][hop])
                hand_on(w, NZ - hop, down[w][hop])
                arriving = [hop, NZ - hop]
            else:
                hand_on(w, hop, up[w][hop])
                arriving = [hop]
            for d in waiting:
                images(d)
            waiting = arriving if w == 1 else []
    for d in waiting:
        images(d)

    def settle(d, carry):
        for dx in range(1, NX):
            term_copy(d, dx).wait_recv()
        return carry

    lax.fori_loop(0, NZ, settle, 0)

    def total(slot, carry):
        out[slot] = out[slot] + (
            taken[0, slot].astype(jnp.float32)
            + taken[1, slot].astype(jnp.float32)
            + taken[2, slot].astype(jnp.float32)
        )
        return carry

    lax.fori_loop(0, out.shape[0], total, 0, unroll=4)

    for w in range(2):
        for way in range(2):
            for hop, k in number:
                ring_copy(w, way, hop, k).wait_send()
    for d in range(1, NZ):
        mate_copy(d).wait_send()
    for j in range(1, MEMBERS):
        table_copy(j).wait_send()

    def sent(d, carry):
        for j in range(1, MEMBERS):
            row_copy(0, d, j).wait_send()
            row_copy(1, d, j).wait_send()
        for dx in range(1, NX):
            term_copy(d, dx).wait_send()
        return carry

    lax.fori_loop(0, NZ, sent, 0)


def gather_kernel(me, tables, found, out, acc):
    acc[...] = jnp.zeros_like(acc)
    column = (MEMBERS + me[0]) * CAP

    def step(i, carry):
        tag = tables[((i // CAP) % MEMBERS) * NZ + i // (MEMBERS * CAP), 0, column + i % CAP]

        @pl.when(tag >= 0)
        def _():
            acc[tag] += found[i]

        return carry

    lax.fori_loop(0, found.shape[0], step, 0)
    out[...] = acc[...].astype(out.dtype)


def image_kernel(tags_ref, left_ref, arrived_ref, out_ref, acc):
    slots = arrived_ref.shape[0]
    acc[...] = jnp.zeros_like(acc)

    def step(i, carry):
        tag = tags_ref[i]

        @pl.when(tag >= 0)
        def _():
            lhs = jnp.concatenate([left_ref[0, tag], left_ref[1, tag]], axis=-1)
            acc[tag] += jnp.dot(lhs, arrived_ref[i], preferred_element_type=jnp.float32)

        return carry

    lax.fori_loop(0, slots, step, 0)
    out_ref[...] = acc[...]


SMEM = pl.BlockSpec(memory_space=pltpu.SMEM)
VMEM = pl.BlockSpec(memory_space=pltpu.VMEM)
ANY = pl.BlockSpec(memory_space=pl.ANY)


def full_exchange(psi_blocks, right_ops, slot_source, left_ops, tags):
    terms, sec_dev, width, _ = left_ops.shape
    inter = (
        jnp.einsum("sij,tsjk->stik", psi_blocks, right_ops, preferred_element_type=jnp.float32)
        .astype(jnp.bfloat16)
        .reshape(sec_dev, terms * width, width)
    )
    packed = jnp.take(inter, slot_source, axis=0, mode="clip")
    arrived = lax.all_to_all(packed, "sector", split_axis=0, concat_axis=0, tiled=True)
    partial = pl.pallas_call(
        image_kernel,
        out_shape=jax.ShapeDtypeStruct((sec_dev, width, width), jnp.float32),
        in_specs=[SMEM, VMEM, VMEM],
        out_specs=VMEM,
        scratch_shapes=[pltpu.VMEM((sec_dev, width, width), jnp.float32)],
        compiler_params=pltpu.CompilerParams(vmem_limit_bytes=48 << 20),
        name="images",
    )(tags, left_ops, arrived)
    parts = lax.all_to_all(
        partial.reshape(sec_dev, NX, width // NX, width), "term", split_axis=1, concat_axis=1
    )
    return jnp.sum(parts, axis=1).astype(jnp.bfloat16)


def ring_exchange(order, table, psi_blocks, right_ops, left_ops):
    terms, sec_dev, width, _ = left_ops.shape
    slots = NZ * MEMBERS * CAP
    rows = width // NX
    dma = pltpu.SemaphoreType.DMA
    pieces = sum(range(1, HOPS + 1))

    def blocks(*lead):
        return pltpu.VMEM((*lead, width, width), jnp.bfloat16)

    wave = [blocks(REACH[h]) for h in (0, 1, 2)] * 2 + [blocks(2 * REACH[3])]
    return pl.pallas_call(
        ring_kernel,
        out_shape=(
            jax.ShapeDtypeStruct((slots, rows, width), jnp.float32),
            jax.ShapeDtypeStruct((MEMBERS, NZ, 1, 128), jnp.int32),
        ),
        in_specs=[SMEM, VMEM, ANY, ANY, ANY],
        out_specs=(VMEM, VMEM),
        scratch_shapes=[
            blocks(sec_dev),
            blocks(terms, sec_dev),
            blocks(terms, sec_dev),
            blocks(sec_dev),
            blocks(sec_dev),
            *wave,
            *wave,
            pltpu.VMEM((2, NZ, MEMBERS, CAP * width, width), jnp.bfloat16),
            pltpu.VMEM((2, NZ, MEMBERS, CAP * width, width), jnp.bfloat16),
            pltpu.VMEM((NX - 1, slots, rows, width), jnp.bfloat16),
            pltpu.VMEM((NX - 1, slots, rows, width), jnp.bfloat16),
            pltpu.VMEM((NZ, 1, 128), jnp.int32),
            pltpu.SMEM((NZ, 1, 128), jnp.int32),
            pltpu.VMEM((MEMBERS, NZ, 1, 128), jnp.int32),
            pltpu.SMEM((MEMBERS, NZ, 1, 128), jnp.int32),
            dma((3,)),
            dma((4,)),
            dma((2, 2, pieces)),
            dma((2, 2, pieces)),
            dma((2, NZ, MEMBERS)),
            dma((2, NZ, MEMBERS)),
            dma((NZ, NX)),
            dma((NZ, NX)),
            dma((NZ,)),
            dma((NZ,)),
            dma((MEMBERS,)),
            dma((MEMBERS,)),
        ],
        compiler_params=pltpu.CompilerParams(
            collective_id=0, has_side_effects=True, vmem_limit_bytes=63 << 20
        ),
        name="ring",
    )(order, table, psi_blocks, right_ops, left_ops)


def local(psi_blocks, right_ops, left_ops, owner_map, left_local):
    sec_dev, width, _ = psi_blocks.shape
    slots = lax.axis_size("sector") * CAP
    mine = lax.axis_index("sector")
    my_c, my_z, my_y = mine % NC, (mine // NC) % NZ, mine // (NC * NZ)
    my_member = my_y * NC + my_c
    owners = owner_map[:, 0]
    ranks = ranks_of(owners)
    position, order, fits = plan_of(owners, my_z)
    table = tables_of(owners, ranks, left_local[:, 0], position, fits, my_z)
    found, tables = ring_exchange(order, table, psi_blocks, right_ops, left_ops)
    tables = tables.reshape(MEMBERS * NZ, 1, 128)
    all_fit = jnp.min(tables[:, 0, 127]) > 0

    def by_ring(found, tables, psi_blocks, right_ops, left_ops):
        return pl.pallas_call(
            gather_kernel,
            out_shape=jax.ShapeDtypeStruct((sec_dev, width // NX, width), jnp.bfloat16),
            in_specs=[SMEM, SMEM, VMEM],
            out_specs=VMEM,
            scratch_shapes=[pltpu.VMEM((sec_dev, width // NX, width), jnp.float32)],
            name="gather",
        )(my_member.reshape(1), tables, found)

    def by_all(found, tables, psi_blocks, right_ops, left_ops):
        slot_id = owners * CAP + ranks
        hot = slot_id[None, :] == lax.broadcasted_iota(jnp.int32, (slots, sec_dev), 0)
        slot_source = jnp.sum(
            jnp.where(hot, lax.broadcasted_iota(jnp.int32, (slots, sec_dev), 1), 0), axis=1
        )
        tags = lax.dynamic_slice_in_dim(
            tables[:, 0], (MEMBERS + my_member) * CAP, CAP, axis=1
        ).reshape(NY, NC, NZ, CAP)
        tags = tags.transpose(0, 2, 1, 3).reshape(slots)
        return full_exchange(psi_blocks, right_ops, slot_source, left_ops, tags)

    return lax.cond(
        all_fit, by_ring, by_all, found, tables, psi_blocks, right_ops, left_ops
    )


def solution(mesh):
    placed = (
        P("sector", None, None),
        P("term", "sector", None, None),
        P("term", "sector", None, None),
        P("sector", None),
        P("sector", None),
    )
    return jax.shard_map(
        local, mesh=mesh, in_specs=placed, out_specs=P("sector", "term", None), check_vma=False
    )
```

```python
import functools

import jax
import jax.numpy as jnp
from jax import lax
from jax.experimental import pallas as pl
from jax.experimental.pallas import tpu as pltpu
from jax.sharding import PartitionSpec as P

MESH = pl.DeviceIdType.MESH
CAP = 2
NY, NZ, NC = 4, 8, 2
NX = 4
MEMBERS = NY * NC
REACH = (33, 24, 16, 7)
HOPS = len(REACH)


def chunk_bounds(hop):
    edges = [0, *reversed(REACH[hop - 1 :])]
    return list(zip(edges[:-1], edges[1:]))


def ranks_of(owners):
    count = owners.shape[-1]
    same = owners[..., :, None] == owners[..., None, :]
    earlier = lax.broadcasted_iota(jnp.int32, (count, count), 0) < lax.broadcasted_iota(
        jnp.int32, (count, count), 1
    )
    return jnp.sum((same & earlier).astype(jnp.int32), axis=-2)


def down_of(row):
    n = row.shape[1]
    same = lax.broadcasted_iota(jnp.int32, (n, n), 0) == lax.broadcasted_iota(jnp.int32, (n, n), 1)
    return jnp.sum(jnp.where(same, row, 0), axis=1, keepdims=True)


def across_of(column):
    n = column.shape[0]
    same = lax.broadcasted_iota(jnp.int32, (n, n), 0) == lax.broadcasted_iota(jnp.int32, (n, n), 1)
    return jnp.sum(jnp.where(same, column, 0), axis=0, keepdims=True)


def count_down(hits):
    return jnp.sum(jnp.where(hits, 1, 0), axis=0, keepdims=True)


def count_across(hits):
    return jnp.sum(jnp.where(hits, 1, 0), axis=1, keepdims=True)


def plan_of(owners, local, z):
    n = owners.shape[1]
    i = lax.broadcasted_iota(jnp.int32, (n, n), 0)
    j = lax.broadcasted_iota(jnp.int32, (n, n), 1)
    owners_down = down_of(owners)
    ranks = count_down((owners_down == owners) & (i < j))
    away = ((owners // NC) % NZ - z + NZ) % NZ
    counts = [count_across(away == d) for d in range(NZ)]
    up = [sum(counts[h:HOPS]) for h in range(1, HOPS)] + [0]
    down = [sum(counts[NZ - h] for h in range(k, HOPS)) for k in range(1, HOPS)] + [0]
    room_up = functools.reduce(jnp.minimum, [REACH[h] - up[h] for h in range(HOPS)])
    room_down = functools.reduce(jnp.minimum, [REACH[h] - down[h] for h in range(HOPS)])
    far_up = jnp.minimum(jnp.maximum(room_up, 0), counts[HOPS])
    fits = jnp.where((room_up >= 0) & (room_down >= counts[HOPS] - far_up), 1, 0)
    opposite = down_of(jnp.where(away == HOPS, 1, 0))
    far_rank = jnp.sum(jnp.where(i < j, opposite, 0), axis=0, keepdims=True)
    signed = jnp.where(
        away == HOPS,
        jnp.where(far_rank < far_up, -HOPS, HOPS),
        jnp.where(away < HOPS, -away, NZ - away),
    )
    key = signed * n + j[:1]
    position = count_down(down_of(key) < key)
    position_down = down_of(position)
    order = jnp.sum(jnp.where(position_down == j, i, 0), axis=0, keepdims=True)

    wide = NZ * MEMBERS * CAP
    entry = lax.broadcasted_iota(jnp.int32, (1, wide), 1)
    mate = entry // (MEMBERS * CAP)
    member = (entry // CAP) % MEMBERS
    goal = ((member // NC) * NZ + mate) * NC + member % NC
    hits = (owners_down == goal) & (down_of(ranks) == entry % CAP)
    ahead = (mate - z + NZ) % NZ
    start, size = jnp.zeros_like(ahead), jnp.full_like(ahead, n)
    for h in range(1, HOPS):
        start = jnp.where(ahead == NZ - h, n - REACH[h - 1], start)
        size = jnp.where((ahead == h) | (ahead == NZ - h), REACH[h - 1], size)
    size = jnp.where(ahead == HOPS, 2 * REACH[-1], size)
    where = jnp.sum(jnp.where(hits, position_down, 0), axis=0, keepdims=True) - start
    where = jnp.where((ahead == HOPS) & (where >= REACH[-1]), where - (n - 2 * REACH[-1]), where)
    where = jnp.minimum(jnp.maximum(where, 0), size - 1)
    tags = jnp.sum(jnp.where(hits, down_of(local) + 1, 0), axis=0, keepdims=True) - 1
    return order, where, tags, jnp.broadcast_to(fits, (1, wide))


def sort_of(tags, slots):
    n = tags.shape[0]
    place = lax.broadcasted_iota(jnp.int32, (n, n), 1)
    tags = jnp.where(tags < 0, n // CAP, tags)
    key = tags * n + lax.broadcasted_iota(jnp.int32, (n, 1), 0)
    earlier = across_of(key) < key
    at = count_across(earlier)
    follows = jnp.where(count_across(earlier & (across_of(tags) == tags)) > 0, 1, 0)
    order = jnp.sum(jnp.where(at == place, slots, 0), axis=0, keepdims=True)
    keep = jnp.sum(jnp.where(at == place, follows, 0), axis=0, keepdims=True)
    last = jnp.maximum(count_down(tags <= place) - 1, 0)
    has = jnp.where(count_down(tags == place) > 0, 1, 0)
    return order, keep, last, has


def ring_kernel(
    owners, local, psi_far, right_far, left_far, out, fit,
    psi, right, left, inter0, inter1,
    up10, up20, up30, down10, down20, down30, far0,
    up11, up21, up31, down11, down21, down31, far1,
    outgoing, arrived, shares, taken, own, runs,
    order_row, order, table, mates, picks, rowmates, tags, line_rows, lines,
    load, local_sem, ring_send, ring_recv, row_send, row_recv, term_send, term_recv,
    mate_send, mate_recv, table_send, table_recv,
):
    count, width = psi.shape[0], psi.shape[1]
    rows = out.shape[1]
    slots = own.shape[0]
    per_source = MEMBERS * CAP
    x = lax.axis_index("term")
    place = lax.axis_index("sector")
    c = place % NC
    z = (place // NC) % NZ
    y = place // (NC * NZ)
    my_member = y * NC + c

    def sector_id(yy, zz, cc):
        return {"sector": (yy * NZ + zz) * NC + cc}

    def member_of(j):
        return (y + j // NC) % NY, (c + j) % NC

    z_up, z_down = (z + 1) % NZ, (z + NZ - 1) % NZ
    loads = [
        pltpu.make_async_copy(psi_far, psi, load.at[0]),
        pltpu.make_async_copy(right_far, right, load.at[1]),
        pltpu.make_async_copy(left_far, left, load.at[2]),
    ]
    for copy in loads:
        copy.start()
    barrier = pltpu.get_barrier_semaphore()
    for d in range(1, NZ):
        pl.semaphore_signal(
            barrier, inc=1, device_id=sector_id(y, (z + d) % NZ, c), device_id_type=MESH
        )
    for j in range(1, MEMBERS):
        yy, cc = member_of(j)
        pl.semaphore_signal(barrier, inc=1, device_id=sector_id(yy, z, cc), device_id_type=MESH)
    for d in range(1, NX):
        pl.semaphore_signal(barrier, inc=1, device_id={"term": (x + d) % NX}, device_id_type=MESH)

    inter = (inter0, inter1)
    up = ((inter0, up10, up20, up30, far0), (inter1, up11, up21, up31, far1))
    down = ((inter0, down10, down20, down30, far0), (inter1, down11, down21, down31, far1))
    reach_far = REACH[-1]
    number = {}
    for hop in range(1, HOPS + 1):
        for k in range(len(chunk_bounds(hop))):
            number[hop, k] = len(number)

    def ring_copy(w, way, hop, k):
        near, end = chunk_bounds(hop)[k]
        size = end - near
        if way == 0:
            source, target, neighbour = up[w][hop - 1], up[w][hop], z_up
            src_at, dst_at = near, near
        else:
            source, target, neighbour = down[w][hop - 1], down[w][hop], z_down
            held = count if hop == 1 else REACH[hop - 2]
            src_at = held - end
            dst_at = REACH[hop - 1] - end + (reach_far if hop == HOPS else 0)
        return pltpu.make_async_remote_copy(
            src_ref=source.at[pl.ds(src_at, size)],
            dst_ref=target.at[pl.ds(dst_at, size)],
            send_sem=ring_send.at[w, way, number[hop, k]],
            recv_sem=ring_recv.at[w, way, number[hop, k]],
            device_id=sector_id(y, neighbour, c),
            device_id_type=MESH,
        )

    def row_copy(w, d, j):
        yy, cc = member_of(j)
        return pltpu.make_async_remote_copy(
            src_ref=outgoing.at[w, d, j],
            dst_ref=arrived.at[w, (z + NZ - d) % NZ, my_member],
            send_sem=row_send.at[w, d, j],
            recv_sem=row_recv.at[w, d, j],
            device_id=sector_id(yy, z, cc),
            device_id_type=MESH,
        )

    def term_copy(d, dx):
        group = pl.ds(((z + NZ - d) % NZ) * per_source, per_source)
        return pltpu.make_async_remote_copy(
            src_ref=shares.at[dx - 1, group],
            dst_ref=taken.at[dx - 1, group],
            send_sem=term_send.at[d, dx],
            recv_sem=term_recv.at[d, dx],
            device_id={"term": (x + dx) % NX},
            device_id_type=MESH,
        )

    def mate_copy(d):
        mate = (z + d) % NZ
        return pltpu.make_async_remote_copy(
            src_ref=table,
            dst_ref=mates.at[z],
            send_sem=mate_send.at[d],
            recv_sem=mate_recv.at[d],
            device_id=sector_id(y, mate, c),
            device_id_type=MESH,
        )

    def table_copy(j):
        yy, cc = member_of(j)
        return pltpu.make_async_remote_copy(
            src_ref=mates,
            dst_ref=rowmates.at[my_member],
            send_sem=table_send.at[j],
            recv_sem=table_recv.at[j],
            device_id=sector_id(yy, z, cc),
            device_id_type=MESH,
        )

    def multiply(p, carry):
        s = order[0, p]
        both = jnp.concatenate([right[0, s], right[1, s]], axis=-1)
        made = jnp.dot(psi[s], both, preferred_element_type=jnp.float32).astype(inter0.dtype)
        inter0[p] = made[:, :width]
        inter1[p] = made[:, width:]
        return carry

    def hand_on(w, d, held):
        source = (z + NZ - d) % NZ

        def one(j, carry):
            yy, cc = member_of(j)
            entry = (z * MEMBERS + yy * NC + cc) * CAP
            outgoing[w, d, j, :width] = held[picks[source, 0, 0, entry]]
            outgoing[w, d, j, width:] = held[picks[source, 0, 0, entry + 1]]
            row_copy(w, d, j).start()
            return carry

        lax.fori_loop(1, MEMBERS, one, 0)
        entry = (z * MEMBERS + my_member) * CAP
        arrived[w, source, my_member, :width] = held[picks[source, 0, 0, entry]]
        arrived[w, source, my_member, width:] = held[picks[source, 0, 0, entry + 1]]

    def images(d):
        source = (z + NZ - d) % NZ

        def landed(j, carry):
            row_copy(0, d, j).wait_recv()
            row_copy(1, d, j).wait_recv()
            return carry

        lax.fori_loop(1, MEMBERS, landed, 0)

        def one(m, carry):
            for r in range(CAP):
                slot = source * per_source + m * CAP + r
                tag = jnp.maximum(tags[m, source, 0, 0, (z * MEMBERS + my_member) * CAP + r], 0)
                lhs = jnp.concatenate(
                    [
                        jnp.concatenate(
                            [left[t, tag, pl.ds(((x + dx) % NX) * rows, rows)] for dx in range(NX)],
                            axis=0,
                        )
                        for t in range(2)
                    ],
                    axis=1,
                )
                rhs = jnp.concatenate(
                    [arrived[t, source, m, r * width : (r + 1) * width] for t in range(2)], axis=0
                )
                image = jnp.dot(lhs, rhs, preferred_element_type=jnp.float32)
                own[slot] = image[:rows]
                for dx in range(1, NX):
                    shares[dx - 1, slot] = image[dx * rows : (dx + 1) * rows].astype(shares.dtype)
            return carry

        lax.fori_loop(0, MEMBERS, one, 0)
        for dx in range(1, NX):
            term_copy(d, dx).start()

    plan = plan_of(owners[...], local[...], z)
    order_row[:, :count] = plan[0]
    to_order = pltpu.make_async_copy(order_row, order, local_sem.at[0])
    to_order.start()
    for k in range(3):
        table[k] = plan[k + 1]
    to_order.wait()
    loads[0].wait()
    loads[1].wait()
    edges = [0, *reversed(REACH)]
    spans = [
        [(edges[k], edges[k + 1]), (count - edges[k + 1], count - edges[k])] for k in range(HOPS)
    ]
    spans[-1] = [(edges[HOPS - 1], count - edges[HOPS - 1])]
    for k in range(HOPS):
        for low, high in spans[k]:
            lax.fori_loop(low, high, multiply, 0, unroll=True)
        if k == 0:
            pl.semaphore_wait(barrier, NZ - 1 + MEMBERS - 1 + NX - 1)
            for d in range(1, NZ):
                mate_copy(d).start()
        ring_copy(0, 0, 1, k).start()
        ring_copy(0, 1, 1, k).start()

    own_table = pltpu.make_async_copy(table, mates.at[z], local_sem.at[1])
    own_table.start()
    own_table.wait()
    for d in range(1, NZ):
        mate_copy(d).wait_recv()
    for j in range(1, MEMBERS):
        table_copy(j).start()
    to_picks = pltpu.make_async_copy(mates, picks, local_sem.at[2])
    to_picks.start()
    own_tables = pltpu.make_async_copy(mates, rowmates.at[my_member], local_sem.at[3])
    own_tables.start()
    to_picks.wait()
    for w in range(2):
        hand_on(w, 0, inter[w])
    own_tables.wait()
    for j in range(1, MEMBERS):
        table_copy(j).wait_recv()
    to_tags = pltpu.make_async_copy(rowmates.at[:, :, pl.ds(1, 1)], tags, local_sem.at[4])
    to_tags.start()
    every = jnp.min(rowmates[:, :, 2, 0], axis=0)
    fit[...] = jnp.broadcast_to(jnp.min(every, axis=0, keepdims=True), fit.shape)
    lane = lax.broadcasted_iota(jnp.int32, (1, 1, slots), 2)
    known = rowmates[:, :, 1, 0]
    mine = [
        jnp.sum(
            jnp.where(lane == (z * MEMBERS + my_member) * CAP + r, known, 0), axis=2, keepdims=True
        ).reshape(MEMBERS * NZ, 1)
        for r in range(CAP)
    ]
    row = lax.broadcasted_iota(jnp.int32, (slots, 1), 0)
    source_of, member_at = row % NZ, (row // NZ) % MEMBERS
    slot_at = source_of * per_source + member_at * CAP + row // (MEMBERS * NZ)
    line = sort_of(jnp.concatenate(mine, axis=0), slot_at)
    for k in range(4):
        line_rows[k] = line[k]
    to_lines = pltpu.make_async_copy(line_rows, lines, local_sem.at[5])
    to_lines.start()
    to_tags.wait()
    to_lines.wait()
    loads[2].wait()

    waiting = [0]
    for w in range(2):
        for hop in range(1, HOPS + 1):
            pieces = len(chunk_bounds(hop))
            for k in range(pieces):
                for way in range(2):
                    ring_copy(w, way, hop, k).wait_recv()
                if k < pieces - 1:
                    between = w == 0 and hop == HOPS - 1
                    if between:
                        for late in range(HOPS - 1):
                            ring_copy(1, 0, 1, late).start()
                            ring_copy(1, 1, 1, late).start()
                    ring_copy(w, 0, hop + 1, k).start()
                    ring_copy(w, 1, hop + 1, k).start()
                    if between:
                        ring_copy(1, 0, 1, HOPS - 1).start()
                        ring_copy(1, 1, 1, HOPS - 1).start()
            if hop < HOPS:
                hand_on(w, hop, up[w][hop])
                hand_on(w, NZ - hop, down[w][hop])
                arriving = [hop, NZ - hop]
            else:
                hand_on(w, hop, up[w][hop])
                arriving = [hop]
            for d in waiting:
                images(d)
            waiting = arriving if w == 1 else []
    for d in waiting:
        images(d)

    def settle(d, carry):
        for dx in range(1, NX):
            term_copy(d, dx).wait_recv()
        return carry

    lax.fori_loop(0, NZ, settle, 0)

    def total(p, run):
        slot = lines[0, 0, p]
        found = own[slot] + (
            taken[0, slot].astype(jnp.float32)
            + taken[1, slot].astype(jnp.float32)
            + taken[2, slot].astype(jnp.float32)
        )
        run = found + lines[1, 0, p].astype(jnp.float32) * run
        runs[p] = run
        return run

    lax.fori_loop(0, slots, total, jnp.zeros(own.shape[1:], jnp.float32), unroll=4)

    def give(l, carry):
        kept = lines[3, 0, l].astype(jnp.float32)
        out[l] = (kept * runs[lines[2, 0, l]]).astype(out.dtype)
        return carry

    lax.fori_loop(0, out.shape[0], give, 0, unroll=4)

    for w in range(2):
        for way in range(2):
            for hop, k in number:
                ring_copy(w, way, hop, k).wait_send()
    for d in range(1, NZ):
        mate_copy(d).wait_send()
    for j in range(1, MEMBERS):
        table_copy(j).wait_send()

    def sent(d, carry):
        for j in range(1, MEMBERS):
            row_copy(0, d, j).wait_send()
            row_copy(1, d, j).wait_send()
        for dx in range(1, NX):
            term_copy(d, dx).wait_send()
        return carry

    lax.fori_loop(0, NZ, sent, 0)


def image_kernel(tags_ref, left_ref, arrived_ref, out_ref, acc):
    slots = arrived_ref.shape[0]
    acc[...] = jnp.zeros_like(acc)

    def step(i, carry):
        tag = tags_ref[i]

        @pl.when(tag >= 0)
        def _():
            lhs = jnp.concatenate([left_ref[0, tag], left_ref[1, tag]], axis=-1)
            acc[tag] += jnp.dot(lhs, arrived_ref[i], preferred_element_type=jnp.float32)

        return carry

    lax.fori_loop(0, slots, step, 0)
    out_ref[...] = acc[...]


SMEM = pl.BlockSpec(memory_space=pltpu.SMEM)
VMEM = pl.BlockSpec(memory_space=pltpu.VMEM)
ANY = pl.BlockSpec(memory_space=pl.ANY)


def full_exchange(psi_blocks, right_ops, slot_source, left_ops, tags):
    terms, sec_dev, width, _ = left_ops.shape
    inter = (
        jnp.einsum("sij,tsjk->stik", psi_blocks, right_ops, preferred_element_type=jnp.float32)
        .astype(jnp.bfloat16)
        .reshape(sec_dev, terms * width, width)
    )
    packed = jnp.take(inter, slot_source, axis=0, mode="clip")
    arrived = lax.all_to_all(packed, "sector", split_axis=0, concat_axis=0, tiled=True)
    partial = pl.pallas_call(
        image_kernel,
        out_shape=jax.ShapeDtypeStruct((sec_dev, width, width), jnp.float32),
        in_specs=[SMEM, VMEM, VMEM],
        out_specs=VMEM,
        scratch_shapes=[pltpu.VMEM((sec_dev, width, width), jnp.float32)],
        compiler_params=pltpu.CompilerParams(vmem_limit_bytes=48 << 20),
        name="images",
    )(tags, left_ops, arrived)
    parts = lax.all_to_all(
        partial.reshape(sec_dev, NX, width // NX, width), "term", split_axis=1, concat_axis=1
    )
    return jnp.sum(parts, axis=1).astype(jnp.bfloat16)


def ring_exchange(owners, local, psi_blocks, right_ops, left_ops):
    terms, sec_dev, width, _ = left_ops.shape
    slots = NZ * MEMBERS * CAP
    rows = width // NX
    dma = pltpu.SemaphoreType.DMA
    pieces = sum(range(1, HOPS + 1))

    def blocks(*lead):
        return pltpu.VMEM((*lead, width, width), jnp.bfloat16)

    wave = [blocks(REACH[h]) for h in (0, 1, 2)] * 2 + [blocks(2 * REACH[3])]
    return pl.pallas_call(
        ring_kernel,
        out_shape=(
            jax.ShapeDtypeStruct((sec_dev, rows, width), jnp.bfloat16),
            jax.ShapeDtypeStruct((8, slots), jnp.int32),
        ),
        in_specs=[VMEM, VMEM, ANY, ANY, ANY],
        out_specs=(VMEM, VMEM),
        scratch_shapes=[
            blocks(sec_dev),
            blocks(terms, sec_dev),
            blocks(terms, sec_dev),
            blocks(sec_dev),
            blocks(sec_dev),
            *wave,
            *wave,
            pltpu.VMEM((2, NZ, MEMBERS, CAP * width, width), jnp.bfloat16),
            pltpu.VMEM((2, NZ, MEMBERS, CAP * width, width), jnp.bfloat16),
            pltpu.VMEM((NX - 1, slots, rows, width), jnp.bfloat16),
            pltpu.VMEM((NX - 1, slots, rows, width), jnp.bfloat16),
            pltpu.VMEM((slots, rows, width), jnp.float32),
            pltpu.VMEM((slots, rows, width), jnp.float32),
            pltpu.VMEM((1, slots), jnp.int32),
            pltpu.SMEM((1, slots), jnp.int32),
            pltpu.VMEM((3, 1, slots), jnp.int32),
            pltpu.VMEM((NZ, 3, 1, slots), jnp.int32),
            pltpu.SMEM((NZ, 3, 1, slots), jnp.int32),
            pltpu.VMEM((MEMBERS, NZ, 3, 1, slots), jnp.int32),
            pltpu.SMEM((MEMBERS, NZ, 1, 1, slots), jnp.int32),
            pltpu.VMEM((4, 1, slots), jnp.int32),
            pltpu.SMEM((4, 1, slots), jnp.int32),
            dma((3,)),
            dma((6,)),
            dma((2, 2, pieces)),
            dma((2, 2, pieces)),
            dma((2, NZ, MEMBERS)),
            dma((2, NZ, MEMBERS)),
            dma((NZ, NX)),
            dma((NZ, NX)),
            dma((NZ,)),
            dma((NZ,)),
            dma((MEMBERS,)),
            dma((MEMBERS,)),
        ],
        compiler_params=pltpu.CompilerParams(
            collective_id=0, has_side_effects=True, vmem_limit_bytes=63 << 20
        ),
        name="ring",
    )(owners, local, psi_blocks, right_ops, left_ops)


def local(psi_blocks, right_ops, left_ops, owner_map, left_local):
    sec_dev, width, _ = psi_blocks.shape
    n_sector = lax.axis_size("sector")
    slots = n_sector * CAP
    found, fit = ring_exchange(
        owner_map.reshape(1, sec_dev), left_local.reshape(1, sec_dev), psi_blocks, right_ops, left_ops
    )

    def by_ring(found, psi_blocks, right_ops, left_ops, owner_map, left_local):
        return found

    def by_all(found, psi_blocks, right_ops, left_ops, owner_map, left_local):
        owners = owner_map[:, 0]
        slot_id = owners * CAP + ranks_of(owners)
        hot = slot_id[None, :] == lax.broadcasted_iota(jnp.int32, (slots, sec_dev), 0)
        slot_source = jnp.sum(
            jnp.where(hot, lax.broadcasted_iota(jnp.int32, (slots, sec_dev), 1), 0), axis=1
        )
        own_tags = jnp.max(jnp.where(hot, left_local[:, 0][None, :], -1), axis=1)
        tags = lax.all_to_all(
            own_tags.reshape(n_sector, CAP), "sector", split_axis=0, concat_axis=0, tiled=True
        ).reshape(slots)
        return full_exchange(psi_blocks, right_ops, slot_source, left_ops, tags)

    return lax.cond(
        fit[0, 0] > 0, by_ring, by_all, found, psi_blocks, right_ops, left_ops, owner_map, left_local
    )


def solution(mesh):
    placed = (
        P("sector", None, None),
        P("term", "sector", None, None),
        P("term", "sector", None, None),
        P("sector", None),
        P("sector", None),
    )
    return jax.shard_map(
        local, mesh=mesh, in_specs=placed, out_specs=P("sector", "term", None), check_vma=False
    )
```

```python
import functools

import jax
import jax.numpy as jnp
from jax import lax
from jax.experimental import pallas as pl
from jax.experimental.pallas import tpu as pltpu
from jax.sharding import PartitionSpec as P

MESH = pl.DeviceIdType.MESH
CAP = 2
NY, NZ, NC = 4, 8, 2
NX = 4
MEMBERS = NY * NC
REACH = (33, 24, 16, 7)
HOPS = len(REACH)


def chunk_bounds(hop):
    edges = [0, *reversed(REACH[hop - 1 :])]
    return list(zip(edges[:-1], edges[1:]))


def ranks_of(owners):
    count = owners.shape[-1]
    same = owners[..., :, None] == owners[..., None, :]
    earlier = lax.broadcasted_iota(jnp.int32, (count, count), 0) < lax.broadcasted_iota(
        jnp.int32, (count, count), 1
    )
    return jnp.sum((same & earlier).astype(jnp.int32), axis=-2)


def down_of(row):
    n = row.shape[1]
    same = lax.broadcasted_iota(jnp.int32, (n, n), 0) == lax.broadcasted_iota(jnp.int32, (n, n), 1)
    return jnp.sum(jnp.where(same, row, 0), axis=1, keepdims=True)


def across_of(column):
    n = column.shape[0]
    same = lax.broadcasted_iota(jnp.int32, (n, n), 0) == lax.broadcasted_iota(jnp.int32, (n, n), 1)
    return jnp.sum(jnp.where(same, column, 0), axis=0, keepdims=True)


def count_down(hits):
    return jnp.sum(jnp.where(hits, 1, 0), axis=0, keepdims=True)


def count_across(hits):
    return jnp.sum(jnp.where(hits, 1, 0), axis=1, keepdims=True)


def plan_of(owners, local, z):
    n = owners.shape[1]
    i = lax.broadcasted_iota(jnp.int32, (n, n), 0)
    j = lax.broadcasted_iota(jnp.int32, (n, n), 1)
    owners_down = down_of(owners)
    ranks = count_down((owners_down == owners) & (i < j))
    away = ((owners // NC) % NZ - z + NZ) % NZ
    counts = [count_across(away == d) for d in range(NZ)]
    up = [sum(counts[h:HOPS]) for h in range(1, HOPS)] + [0]
    down = [sum(counts[NZ - h] for h in range(k, HOPS)) for k in range(1, HOPS)] + [0]
    room_up = functools.reduce(jnp.minimum, [REACH[h] - up[h] for h in range(HOPS)])
    room_down = functools.reduce(jnp.minimum, [REACH[h] - down[h] for h in range(HOPS)])
    far_up = jnp.minimum(jnp.maximum(room_up, 0), counts[HOPS])
    fits = jnp.where((room_up >= 0) & (room_down >= counts[HOPS] - far_up), 1, 0)
    opposite = down_of(jnp.where(away == HOPS, 1, 0))
    far_rank = jnp.sum(jnp.where(i < j, opposite, 0), axis=0, keepdims=True)
    signed = jnp.where(
        away == HOPS,
        jnp.where(far_rank < far_up, -HOPS, HOPS),
        jnp.where(away < HOPS, -away, NZ - away),
    )
    key = signed * n + j[:1]
    position = count_down(down_of(key) < key)
    position_down = down_of(position)
    order = jnp.sum(jnp.where(position_down == j, i, 0), axis=0, keepdims=True)

    wide = NZ * MEMBERS * CAP
    entry = lax.broadcasted_iota(jnp.int32, (1, wide), 1)
    mate = entry // (MEMBERS * CAP)
    member = (entry // CAP) % MEMBERS
    goal = ((member // NC) * NZ + mate) * NC + member % NC
    hits = (owners_down == goal) & (down_of(ranks) == entry % CAP)
    ahead = (mate - z + NZ) % NZ
    start, size = jnp.zeros_like(ahead), jnp.full_like(ahead, n)
    for h in range(1, HOPS):
        start = jnp.where(ahead == NZ - h, n - REACH[h - 1], start)
        size = jnp.where((ahead == h) | (ahead == NZ - h), REACH[h - 1], size)
    size = jnp.where(ahead == HOPS, 2 * REACH[-1], size)
    where = jnp.sum(jnp.where(hits, position_down, 0), axis=0, keepdims=True) - start
    where = jnp.where((ahead == HOPS) & (where >= REACH[-1]), where - (n - 2 * REACH[-1]), where)
    where = jnp.minimum(jnp.maximum(where, 0), size - 1)
    tags = jnp.sum(jnp.where(hits, down_of(local) + 1, 0), axis=0, keepdims=True) - 1
    return order, where, tags, jnp.broadcast_to(fits, (1, wide))


def sort_of(tags, slots):
    n = tags.shape[0]
    place = lax.broadcasted_iota(jnp.int32, (n, n), 1)
    tags = jnp.where(tags < 0, n // CAP, tags)
    key = tags * n + lax.broadcasted_iota(jnp.int32, (n, 1), 0)
    earlier = across_of(key) < key
    at = count_across(earlier)
    follows = jnp.where(count_across(earlier & (across_of(tags) == tags)) > 0, 1, 0)
    order = jnp.sum(jnp.where(at == place, slots, 0), axis=0, keepdims=True)
    keep = jnp.sum(jnp.where(at == place, follows, 0), axis=0, keepdims=True)
    last = jnp.maximum(count_down(tags <= place) - 1, 0)
    has = jnp.where(count_down(tags == place) > 0, 1, 0)
    return order, keep, last, has


def ring_kernel(
    owners, local, psi_far, right_far, left_far, out, fit,
    psi, right, left, inter0, inter1,
    up10, up20, up30, down10, down20, down30, far0,
    up11, up21, up31, down11, down21, down31, far1,
    outgoing, arrived, shares, taken, own, runs,
    order_row, order, table, mates, picks, rowmates, tags, line_rows, lines,
    load, local_sem, ring_send, ring_recv, row_send, row_recv, term_send, term_recv,
    mate_send, mate_recv, table_send, table_recv,
):
    count, width = psi.shape[0], psi.shape[1]
    rows = out.shape[1]
    slots = own.shape[0]
    per_source = MEMBERS * CAP
    x = lax.axis_index("term")
    place = lax.axis_index("sector")
    c = place % NC
    z = (place // NC) % NZ
    y = place // (NC * NZ)
    my_member = y * NC + c

    def sector_id(yy, zz, cc):
        return {"sector": (yy * NZ + zz) * NC + cc}

    def member_of(j):
        return (y + j // NC) % NY, (c + j) % NC

    z_up, z_down = (z + 1) % NZ, (z + NZ - 1) % NZ
    loads = [
        pltpu.make_async_copy(psi_far, psi, load.at[0]),
        pltpu.make_async_copy(right_far, right, load.at[1]),
        pltpu.make_async_copy(left_far, left, load.at[2]),
    ]
    for copy in loads:
        copy.start()
    barrier = pltpu.get_barrier_semaphore()
    for d in range(1, NZ):
        pl.semaphore_signal(
            barrier, inc=1, device_id=sector_id(y, (z + d) % NZ, c), device_id_type=MESH
        )
    for j in range(1, MEMBERS):
        yy, cc = member_of(j)
        pl.semaphore_signal(barrier, inc=1, device_id=sector_id(yy, z, cc), device_id_type=MESH)
    for d in range(1, NX):
        pl.semaphore_signal(barrier, inc=1, device_id={"term": (x + d) % NX}, device_id_type=MESH)

    inter = (inter0, inter1)
    up = ((inter0, up10, up20, up30, far0), (inter1, up11, up21, up31, far1))
    down = ((inter0, down10, down20, down30, far0), (inter1, down11, down21, down31, far1))
    reach_far = REACH[-1]
    number = {}
    for hop in range(1, HOPS + 1):
        for k in range(len(chunk_bounds(hop))):
            number[hop, k] = len(number)

    def ring_copy(w, way, hop, k):
        near, end = chunk_bounds(hop)[k]
        size = end - near
        if way == 0:
            source, target, neighbour = up[w][hop - 1], up[w][hop], z_up
            src_at, dst_at = near, near
        else:
            source, target, neighbour = down[w][hop - 1], down[w][hop], z_down
            held = count if hop == 1 else REACH[hop - 2]
            src_at = held - end
            dst_at = REACH[hop - 1] - end + (reach_far if hop == HOPS else 0)
        return pltpu.make_async_remote_copy(
            src_ref=source.at[pl.ds(src_at, size)],
            dst_ref=target.at[pl.ds(dst_at, size)],
            send_sem=ring_send.at[w, way, number[hop, k]],
            recv_sem=ring_recv.at[w, way, number[hop, k]],
            device_id=sector_id(y, neighbour, c),
            device_id_type=MESH,
        )

    def row_copy(w, d, j):
        yy, cc = member_of(j)
        return pltpu.make_async_remote_copy(
            src_ref=outgoing.at[w, d, j],
            dst_ref=arrived.at[w, (z + NZ - d) % NZ, my_member],
            send_sem=row_send.at[w, d, j],
            recv_sem=row_recv.at[w, d, j],
            device_id=sector_id(yy, z, cc),
            device_id_type=MESH,
        )

    def term_copy(d, dx):
        group = pl.ds(((z + NZ - d) % NZ) * per_source, per_source)
        return pltpu.make_async_remote_copy(
            src_ref=shares.at[dx - 1, group],
            dst_ref=taken.at[dx - 1, group],
            send_sem=term_send.at[d, dx],
            recv_sem=term_recv.at[d, dx],
            device_id={"term": (x + dx) % NX},
            device_id_type=MESH,
        )

    def mate_copy(d):
        mate = (z + d) % NZ
        return pltpu.make_async_remote_copy(
            src_ref=table,
            dst_ref=mates.at[z],
            send_sem=mate_send.at[d],
            recv_sem=mate_recv.at[d],
            device_id=sector_id(y, mate, c),
            device_id_type=MESH,
        )

    def table_copy(j):
        yy, cc = member_of(j)
        return pltpu.make_async_remote_copy(
            src_ref=mates,
            dst_ref=rowmates.at[my_member],
            send_sem=table_send.at[j],
            recv_sem=table_recv.at[j],
            device_id=sector_id(yy, z, cc),
            device_id_type=MESH,
        )

    def multiply(p, carry):
        s = order[0, p]
        both = jnp.concatenate([right[0, s], right[1, s]], axis=-1)
        made = jnp.dot(psi[s], both, preferred_element_type=jnp.float32).astype(inter0.dtype)
        inter0[p] = made[:, :width]
        inter1[p] = made[:, width:]
        return carry

    def hand_on(w, d, held):
        source = (z + NZ - d) % NZ

        def one(j, carry):
            yy, cc = member_of(j)
            entry = (z * MEMBERS + yy * NC + cc) * CAP
            outgoing[w, d, j, :width] = held[picks[source, 0, 0, entry]]
            outgoing[w, d, j, width:] = held[picks[source, 0, 0, entry + 1]]
            row_copy(w, d, j).start()
            return carry

        lax.fori_loop(1, MEMBERS, one, 0)
        entry = (z * MEMBERS + my_member) * CAP
        arrived[w, source, my_member, :width] = held[picks[source, 0, 0, entry]]
        arrived[w, source, my_member, width:] = held[picks[source, 0, 0, entry + 1]]

    def images(d):
        source = (z + NZ - d) % NZ

        def landed(j, carry):
            row_copy(0, d, j).wait_recv()
            row_copy(1, d, j).wait_recv()
            return carry

        lax.fori_loop(1, MEMBERS, landed, 0)

        def one(m, carry):
            for r in range(CAP):
                slot = source * per_source + m * CAP + r
                tag = jnp.maximum(tags[m, source, 0, 0, (z * MEMBERS + my_member) * CAP + r], 0)
                lhs = jnp.concatenate(
                    [
                        jnp.concatenate(
                            [left[t, tag, pl.ds(((x + dx) % NX) * rows, rows)] for dx in range(NX)],
                            axis=0,
                        )
                        for t in range(2)
                    ],
                    axis=1,
                )
                rhs = jnp.concatenate(
                    [arrived[t, source, m, r * width : (r + 1) * width] for t in range(2)], axis=0
                )
                image = jnp.dot(lhs, rhs, preferred_element_type=jnp.float32)
                own[slot] = image[:rows]
                for dx in range(1, NX):
                    shares[dx - 1, slot] = image[dx * rows : (dx + 1) * rows].astype(shares.dtype)
            return carry

        lax.fori_loop(0, MEMBERS, one, 0, unroll=4)
        for dx in range(1, NX):
            term_copy(d, dx).start()

    plan = plan_of(owners[...], local[...], z)
    order_row[:, :count] = plan[0]
    to_order = pltpu.make_async_copy(order_row, order, local_sem.at[0])
    to_order.start()
    for k in range(3):
        table[k] = plan[k + 1]
    to_order.wait()
    loads[0].wait()
    loads[1].wait()
    edges = [0, *reversed(REACH)]
    spans = [
        [(edges[k], edges[k + 1]), (count - edges[k + 1], count - edges[k])] for k in range(HOPS)
    ]
    spans[-1] = [(edges[HOPS - 1], count - edges[HOPS - 1])]
    for k in range(HOPS):
        for low, high in spans[k]:
            lax.fori_loop(low, high, multiply, 0, unroll=True)
        if k == 0:
            pl.semaphore_wait(barrier, NZ - 1 + MEMBERS - 1 + NX - 1)
            for d in range(1, NZ):
                mate_copy(d).start()
        ring_copy(0, 0, 1, k).start()
        ring_copy(0, 1, 1, k).start()

    own_table = pltpu.make_async_copy(table, mates.at[z], local_sem.at[1])
    own_table.start()
    own_table.wait()
    for d in range(1, NZ):
        mate_copy(d).wait_recv()
    for j in range(1, MEMBERS):
        table_copy(j).start()
    to_picks = pltpu.make_async_copy(mates, picks, local_sem.at[2])
    to_picks.start()
    own_tables = pltpu.make_async_copy(mates, rowmates.at[my_member], local_sem.at[3])
    own_tables.start()
    to_picks.wait()
    for w in range(2):
        hand_on(w, 0, inter[w])
    own_tables.wait()
    for j in range(1, MEMBERS):
        table_copy(j).wait_recv()
    to_tags = pltpu.make_async_copy(rowmates.at[:, :, pl.ds(1, 1)], tags, local_sem.at[4])
    to_tags.start()
    every = jnp.min(rowmates[:, :, 2, 0], axis=0)
    line_rows[4] = jnp.min(every, axis=0, keepdims=True)
    lane = lax.broadcasted_iota(jnp.int32, (1, 1, slots), 2)
    known = rowmates[:, :, 1, 0]
    mine = [
        jnp.sum(
            jnp.where(lane == (z * MEMBERS + my_member) * CAP + r, known, 0), axis=2, keepdims=True
        ).reshape(MEMBERS * NZ, 1)
        for r in range(CAP)
    ]
    row = lax.broadcasted_iota(jnp.int32, (slots, 1), 0)
    source_of, member_at = row % NZ, (row // NZ) % MEMBERS
    slot_at = source_of * per_source + member_at * CAP + row // (MEMBERS * NZ)
    line = sort_of(jnp.concatenate(mine, axis=0), slot_at)
    for k in range(4):
        line_rows[k] = line[k]
    to_lines = pltpu.make_async_copy(line_rows, lines, local_sem.at[5])
    to_lines.start()
    to_tags.wait()
    to_lines.wait()
    fit[0] = lines[4, 0, 0]
    loads[2].wait()

    early = {(0, 2, 0): [0], (1, 2, 0): [1], (1, 2, 1): [NZ - 1], (1, 3, 0): [2], (1, 4, 0): [NZ - 2]}
    for w in range(2):
        for hop in range(1, HOPS + 1):
            pieces = len(chunk_bounds(hop))
            for k in range(pieces):
                for way in range(2):
                    ring_copy(w, way, hop, k).wait_recv()
                if k < pieces - 1:
                    between = w == 0 and hop == HOPS - 1
                    if between:
                        for late in range(HOPS - 1):
                            ring_copy(1, 0, 1, late).start()
                            ring_copy(1, 1, 1, late).start()
                    ring_copy(w, 0, hop + 1, k).start()
                    ring_copy(w, 1, hop + 1, k).start()
                    if between:
                        ring_copy(1, 0, 1, HOPS - 1).start()
                        ring_copy(1, 1, 1, HOPS - 1).start()
                    for d in early.get((w, hop, k), ()):
                        images(d)
            hand_on(w, hop, up[w][hop])
            if hop < HOPS:
                hand_on(w, NZ - hop, down[w][hop])
            if k == pieces - 1:
                for d in early.get((w, hop, k), ()):
                    images(d)
    for d in (HOPS - 1, NZ - HOPS + 1, HOPS):
        images(d)

    def settle(d):
        for dx in range(1, NX):
            term_copy(d, dx).wait_recv()
        first = ((z + NZ - d) % NZ) * per_source

        def add(i, carry):
            slot = first + i
            own[slot] += (
                taken[0, slot].astype(jnp.float32)
                + taken[1, slot].astype(jnp.float32)
                + taken[2, slot].astype(jnp.float32)
            )
            return carry

        lax.fori_loop(0, per_source, add, 0, unroll=4)

    for d in (0, 1, NZ - 1, 2, NZ - 2, HOPS - 1, NZ - HOPS + 1, HOPS):
        settle(d)

    def total(p, run):
        run = own[lines[0, 0, p]] + lines[1, 0, p].astype(jnp.float32) * run
        runs[p] = run
        return run

    lax.fori_loop(0, slots, total, jnp.zeros(own.shape[1:], jnp.float32), unroll=8)

    def give(l, carry):
        kept = lines[3, 0, l].astype(jnp.float32)
        out[l] = (kept * runs[lines[2, 0, l]]).astype(out.dtype)
        return carry

    lax.fori_loop(0, out.shape[0], give, 0, unroll=8)

    for w in range(2):
        for way in range(2):
            for hop, k in number:
                ring_copy(w, way, hop, k).wait_send()
    for d in range(1, NZ):
        mate_copy(d).wait_send()
    for j in range(1, MEMBERS):
        table_copy(j).wait_send()

    def sent(d, carry):
        for j in range(1, MEMBERS):
            row_copy(0, d, j).wait_send()
            row_copy(1, d, j).wait_send()
        for dx in range(1, NX):
            term_copy(d, dx).wait_send()
        return carry

    lax.fori_loop(0, NZ, sent, 0)


def image_kernel(tags_ref, left_ref, arrived_ref, out_ref, acc):
    slots = arrived_ref.shape[0]
    acc[...] = jnp.zeros_like(acc)

    def step(i, carry):
        tag = tags_ref[i]

        @pl.when(tag >= 0)
        def _():
            lhs = jnp.concatenate([left_ref[0, tag], left_ref[1, tag]], axis=-1)
            acc[tag] += jnp.dot(lhs, arrived_ref[i], preferred_element_type=jnp.float32)

        return carry

    lax.fori_loop(0, slots, step, 0)
    out_ref[...] = acc[...]


SMEM = pl.BlockSpec(memory_space=pltpu.SMEM)
VMEM = pl.BlockSpec(memory_space=pltpu.VMEM)
ANY = pl.BlockSpec(memory_space=pl.ANY)


def full_exchange(psi_blocks, right_ops, slot_source, left_ops, tags):
    terms, sec_dev, width, _ = left_ops.shape
    inter = (
        jnp.einsum("sij,tsjk->stik", psi_blocks, right_ops, preferred_element_type=jnp.float32)
        .astype(jnp.bfloat16)
        .reshape(sec_dev, terms * width, width)
    )
    packed = jnp.take(inter, slot_source, axis=0, mode="clip")
    arrived = lax.all_to_all(packed, "sector", split_axis=0, concat_axis=0, tiled=True)
    partial = pl.pallas_call(
        image_kernel,
        out_shape=jax.ShapeDtypeStruct((sec_dev, width, width), jnp.float32),
        in_specs=[SMEM, VMEM, VMEM],
        out_specs=VMEM,
        scratch_shapes=[pltpu.VMEM((sec_dev, width, width), jnp.float32)],
        compiler_params=pltpu.CompilerParams(vmem_limit_bytes=48 << 20),
        name="images",
    )(tags, left_ops, arrived)
    parts = lax.all_to_all(
        partial.reshape(sec_dev, NX, width // NX, width), "term", split_axis=1, concat_axis=1
    )
    return jnp.sum(parts, axis=1).astype(jnp.bfloat16)


def ring_exchange(owners, local, psi_blocks, right_ops, left_ops):
    terms, sec_dev, width, _ = left_ops.shape
    slots = NZ * MEMBERS * CAP
    rows = width // NX
    dma = pltpu.SemaphoreType.DMA
    pieces = sum(range(1, HOPS + 1))

    def blocks(*lead):
        return pltpu.VMEM((*lead, width, width), jnp.bfloat16)

    wave = [blocks(REACH[h]) for h in (0, 1, 2)] * 2 + [blocks(2 * REACH[3])]
    return pl.pallas_call(
        ring_kernel,
        out_shape=(
            jax.ShapeDtypeStruct((sec_dev, rows, width), jnp.bfloat16),
            jax.ShapeDtypeStruct((1,), jnp.int32),
        ),
        in_specs=[VMEM, VMEM, ANY, ANY, ANY],
        out_specs=(VMEM, SMEM),
        scratch_shapes=[
            blocks(sec_dev),
            blocks(terms, sec_dev),
            blocks(terms, sec_dev),
            blocks(sec_dev),
            blocks(sec_dev),
            *wave,
            *wave,
            pltpu.VMEM((2, NZ, MEMBERS, CAP * width, width), jnp.bfloat16),
            pltpu.VMEM((2, NZ, MEMBERS, CAP * width, width), jnp.bfloat16),
            pltpu.VMEM((NX - 1, slots, rows, width), jnp.bfloat16),
            pltpu.VMEM((NX - 1, slots, rows, width), jnp.bfloat16),
            pltpu.VMEM((slots, rows, width), jnp.float32),
            pltpu.VMEM((slots, rows, width), jnp.float32),
            pltpu.VMEM((1, slots), jnp.int32),
            pltpu.SMEM((1, slots), jnp.int32),
            pltpu.VMEM((3, 1, slots), jnp.int32),
            pltpu.VMEM((NZ, 3, 1, slots), jnp.int32),
            pltpu.SMEM((NZ, 3, 1, slots), jnp.int32),
            pltpu.VMEM((MEMBERS, NZ, 3, 1, slots), jnp.int32),
            pltpu.SMEM((MEMBERS, NZ, 1, 1, slots), jnp.int32),
            pltpu.VMEM((5, 1, slots), jnp.int32),
            pltpu.SMEM((5, 1, slots), jnp.int32),
            dma((3,)),
            dma((6,)),
            dma((2, 2, pieces)),
            dma((2, 2, pieces)),
            dma((2, NZ, MEMBERS)),
            dma((2, NZ, MEMBERS)),
            dma((NZ, NX)),
            dma((NZ, NX)),
            dma((NZ,)),
            dma((NZ,)),
            dma((MEMBERS,)),
            dma((MEMBERS,)),
        ],
        compiler_params=pltpu.CompilerParams(
            collective_id=0, has_side_effects=True, vmem_limit_bytes=63 << 20
        ),
        name="ring",
    )(owners, local, psi_blocks, right_ops, left_ops)


def local(psi_blocks, right_ops, left_ops, owner_map, left_local):
    sec_dev, width, _ = psi_blocks.shape
    n_sector = lax.axis_size("sector")
    slots = n_sector * CAP
    found, fit = ring_exchange(
        owner_map.reshape(1, sec_dev), left_local.reshape(1, sec_dev), psi_blocks, right_ops, left_ops
    )

    def by_ring(found, psi_blocks, right_ops, left_ops, owner_map, left_local):
        return found

    def by_all(found, psi_blocks, right_ops, left_ops, owner_map, left_local):
        owners = owner_map[:, 0]
        slot_id = owners * CAP + ranks_of(owners)
        hot = slot_id[None, :] == lax.broadcasted_iota(jnp.int32, (slots, sec_dev), 0)
        slot_source = jnp.sum(
            jnp.where(hot, lax.broadcasted_iota(jnp.int32, (slots, sec_dev), 1), 0), axis=1
        )
        own_tags = jnp.max(jnp.where(hot, left_local[:, 0][None, :], -1), axis=1)
        tags = lax.all_to_all(
            own_tags.reshape(n_sector, CAP), "sector", split_axis=0, concat_axis=0, tiled=True
        ).reshape(slots)
        return full_exchange(psi_blocks, right_ops, slot_source, left_ops, tags)

    return lax.cond(
        fit[0] > 0, by_ring, by_all, found, psi_blocks, right_ops, left_ops, owner_map, left_local
    )


def solution(mesh):
    placed = (
        P("sector", None, None),
        P("term", "sector", None, None),
        P("term", "sector", None, None),
        P("sector", None),
        P("sector", None),
    )
    return jax.shard_map(
        local, mesh=mesh, in_specs=placed, out_specs=P("sector", "term", None), check_vma=False
    )
```

```python
import functools

import jax
import jax.numpy as jnp
from jax import lax
from jax.experimental import pallas as pl
from jax.experimental.pallas import tpu as pltpu
from jax.sharding import PartitionSpec as P

MESH = pl.DeviceIdType.MESH
CAP = 2
NY, NZ, NC = 4, 8, 2
NX = 4
MEMBERS = NY * NC
REACH = (33, 24, 16, 7)
HOPS = len(REACH)
WAVES = 3
HALVES = ((0,), (1, 2))


def chunk_bounds(hop):
    edges = [0, *reversed(REACH[hop - 1 :])]
    return list(zip(edges[:-1], edges[1:]))


def ranks_of(owners):
    count = owners.shape[-1]
    same = owners[..., :, None] == owners[..., None, :]
    earlier = lax.broadcasted_iota(jnp.int32, (count, count), 0) < lax.broadcasted_iota(
        jnp.int32, (count, count), 1
    )
    return jnp.sum((same & earlier).astype(jnp.int32), axis=-2)


def down_of(row):
    n = row.shape[1]
    same = lax.broadcasted_iota(jnp.int32, (n, n), 0) == lax.broadcasted_iota(jnp.int32, (n, n), 1)
    return jnp.sum(jnp.where(same, row, 0), axis=1, keepdims=True)


def across_of(column):
    n = column.shape[0]
    same = lax.broadcasted_iota(jnp.int32, (n, n), 0) == lax.broadcasted_iota(jnp.int32, (n, n), 1)
    return jnp.sum(jnp.where(same, column, 0), axis=0, keepdims=True)


def count_down(hits):
    return jnp.sum(jnp.where(hits, 1, 0), axis=0, keepdims=True)


def count_across(hits):
    return jnp.sum(jnp.where(hits, 1, 0), axis=1, keepdims=True)


def plan_of(owners, local, z):
    n = owners.shape[1]
    i = lax.broadcasted_iota(jnp.int32, (n, n), 0)
    j = lax.broadcasted_iota(jnp.int32, (n, n), 1)
    owners_down = down_of(owners)
    ranks = count_down((owners_down == owners) & (i < j))
    away = ((owners // NC) % NZ - z + NZ) % NZ
    counts = [count_across(away == d) for d in range(NZ)]
    up = [sum(counts[h:HOPS]) for h in range(1, HOPS)] + [0]
    down = [sum(counts[NZ - h] for h in range(k, HOPS)) for k in range(1, HOPS)] + [0]
    room_up = functools.reduce(jnp.minimum, [REACH[h] - up[h] for h in range(HOPS)])
    room_down = functools.reduce(jnp.minimum, [REACH[h] - down[h] for h in range(HOPS)])
    far_up = jnp.minimum(jnp.maximum(room_up, 0), counts[HOPS])
    fits = jnp.where((room_up >= 0) & (room_down >= counts[HOPS] - far_up), 1, 0)
    opposite = down_of(jnp.where(away == HOPS, 1, 0))
    far_rank = jnp.sum(jnp.where(i < j, opposite, 0), axis=0, keepdims=True)
    signed = jnp.where(
        away == HOPS,
        jnp.where(far_rank < far_up, -HOPS, HOPS),
        jnp.where(away < HOPS, -away, NZ - away),
    )
    key = signed * n + j[:1]
    position = count_down(down_of(key) < key)
    position_down = down_of(position)
    order = jnp.sum(jnp.where(position_down == j, i, 0), axis=0, keepdims=True)

    wide = NZ * MEMBERS * CAP
    entry = lax.broadcasted_iota(jnp.int32, (1, wide), 1)
    mate = entry // (MEMBERS * CAP)
    member = (entry // CAP) % MEMBERS
    goal = ((member // NC) * NZ + mate) * NC + member % NC
    hits = (owners_down == goal) & (down_of(ranks) == entry % CAP)
    ahead = (mate - z + NZ) % NZ
    start, size = jnp.zeros_like(ahead), jnp.full_like(ahead, n)
    for h in range(1, HOPS):
        start = jnp.where(ahead == NZ - h, n - REACH[h - 1], start)
        size = jnp.where((ahead == h) | (ahead == NZ - h), REACH[h - 1], size)
    size = jnp.where(ahead == HOPS, 2 * REACH[-1], size)
    where = jnp.sum(jnp.where(hits, position_down, 0), axis=0, keepdims=True) - start
    where = jnp.where((ahead == HOPS) & (where >= REACH[-1]), where - (n - 2 * REACH[-1]), where)
    where = jnp.minimum(jnp.maximum(where, 0), size - 1)
    tags = jnp.sum(jnp.where(hits, down_of(local) + 1, 0), axis=0, keepdims=True) - 1
    return order, where, tags, jnp.broadcast_to(fits, (1, wide))


def sort_of(tags, slots):
    n = tags.shape[0]
    place = lax.broadcasted_iota(jnp.int32, (n, n), 1)
    tags = jnp.where(tags < 0, n // CAP, tags)
    key = tags * n + lax.broadcasted_iota(jnp.int32, (n, 1), 0)
    earlier = across_of(key) < key
    at = count_across(earlier)
    follows = jnp.where(count_across(earlier & (across_of(tags) == tags)) > 0, 1, 0)
    order = jnp.sum(jnp.where(at == place, slots, 0), axis=0, keepdims=True)
    keep = jnp.sum(jnp.where(at == place, follows, 0), axis=0, keepdims=True)
    last = jnp.maximum(count_down(tags <= place) - 1, 0)
    has = jnp.where(count_down(tags == place) > 0, 1, 0)
    return order, keep, last, has


def ring_kernel(owners, local, psi_far, right_far, left_far, out, fit, psi, right, left, *refs):
    refs = list(refs)

    def take(number):
        taken_refs = refs[:number]
        del refs[:number]
        return taken_refs

    inter = take(WAVES)
    up, down = [], []
    for w in range(WAVES):
        up1, up2, up3, down1, down2, down3, far = take(7)
        up.append((inter[w], up1, up2, up3, far))
        down.append((inter[w], down1, down2, down3, far))
    outgoing, arrived = take(WAVES), take(WAVES)
    shares, taken, own, full, runs = take(5)
    order_row, order, table, mates, picks, rowmates, tags, line_rows, lines = take(9)
    load, local_sem, ring_send, ring_recv, row_send, row_recv, term_send, term_recv = take(8)
    mate_send, mate_recv, table_send, table_recv = take(4)
    count, width = psi.shape[0], psi.shape[1]
    rows = out.shape[1]
    slots = full.shape[0]
    half = width // 2
    per_source = MEMBERS * CAP
    x = lax.axis_index("term")
    place = lax.axis_index("sector")
    c = place % NC
    z = (place // NC) % NZ
    y = place // (NC * NZ)
    my_member = y * NC + c

    def sector_id(yy, zz, cc):
        return {"sector": (yy * NZ + zz) * NC + cc}

    def member_of(j):
        return (y + j // NC) % NY, (c + j) % NC

    z_up, z_down = (z + 1) % NZ, (z + NZ - 1) % NZ
    loads = [
        pltpu.make_async_copy(psi_far, psi, load.at[0]),
        pltpu.make_async_copy(right_far, right, load.at[1]),
        pltpu.make_async_copy(left_far, left, load.at[2]),
    ]
    for copy in loads:
        copy.start()
    barrier = pltpu.get_barrier_semaphore()
    for d in range(1, NZ):
        pl.semaphore_signal(
            barrier, inc=1, device_id=sector_id(y, (z + d) % NZ, c), device_id_type=MESH
        )
    for j in range(1, MEMBERS):
        yy, cc = member_of(j)
        pl.semaphore_signal(barrier, inc=1, device_id=sector_id(yy, z, cc), device_id_type=MESH)
    for d in range(1, NX):
        pl.semaphore_signal(barrier, inc=1, device_id={"term": (x + d) % NX}, device_id_type=MESH)

    reach_far = REACH[-1]
    number = {}
    for hop in range(1, HOPS + 1):
        for k in range(len(chunk_bounds(hop))):
            number[hop, k] = len(number)

    def ring_copy(w, way, hop, k):
        near, end = chunk_bounds(hop)[k]
        size = end - near
        if way == 0:
            source, target, neighbour = up[w][hop - 1], up[w][hop], z_up
            src_at, dst_at = near, near
        else:
            source, target, neighbour = down[w][hop - 1], down[w][hop], z_down
            held = count if hop == 1 else REACH[hop - 2]
            src_at = held - end
            dst_at = REACH[hop - 1] - end + (reach_far if hop == HOPS else 0)
        return pltpu.make_async_remote_copy(
            src_ref=source.at[pl.ds(src_at, size)],
            dst_ref=target.at[pl.ds(dst_at, size)],
            send_sem=ring_send.at[w, way, number[hop, k]],
            recv_sem=ring_recv.at[w, way, number[hop, k]],
            device_id=sector_id(y, neighbour, c),
            device_id_type=MESH,
        )

    def row_copy(w, d, j):
        yy, cc = member_of(j)
        return pltpu.make_async_remote_copy(
            src_ref=outgoing[w].at[d, j],
            dst_ref=arrived[w].at[(z + NZ - d) % NZ, my_member],
            send_sem=row_send.at[w, d, j],
            recv_sem=row_recv.at[w, d, j],
            device_id=sector_id(yy, z, cc),
            device_id_type=MESH,
        )

    def term_copy(h, d, dx):
        group = pl.ds(((z + NZ - d) % NZ) * MEMBERS, MEMBERS)
        return pltpu.make_async_remote_copy(
            src_ref=shares.at[h, dx - 1, group],
            dst_ref=taken.at[h, dx - 1, group],
            send_sem=term_send.at[h, d, dx],
            recv_sem=term_recv.at[h, d, dx],
            device_id={"term": (x + dx) % NX},
            device_id_type=MESH,
        )

    def mate_copy(d):
        mate = (z + d) % NZ
        return pltpu.make_async_remote_copy(
            src_ref=table,
            dst_ref=mates.at[z],
            send_sem=mate_send.at[d],
            recv_sem=mate_recv.at[d],
            device_id=sector_id(y, mate, c),
            device_id_type=MESH,
        )

    def table_copy(j):
        yy, cc = member_of(j)
        return pltpu.make_async_remote_copy(
            src_ref=mates,
            dst_ref=rowmates.at[my_member],
            send_sem=table_send.at[j],
            recv_sem=table_recv.at[j],
            device_id=sector_id(yy, z, cc),
            device_id_type=MESH,
        )

    low = lax.broadcasted_iota(jnp.int32, (width, width), 1) < half
    low_rows = lax.broadcasted_iota(jnp.int32, (rows, width), 1) < half

    def turned(value):
        return pltpu.roll(value, half, 1)

    def multiply(p, carry):
        s = order[0, p]
        both = jnp.concatenate([right[0, s], right[1, s]], axis=-1)
        made = jnp.dot(psi[s], both, preferred_element_type=jnp.float32)
        one, two = made[:, :width], made[:, width:]
        inter[0][p] = jnp.where(low, one, turned(two)).astype(jnp.bfloat16)
        late = jnp.where(low, turned(one), two).astype(jnp.bfloat16)
        inter[1][p] = late[:half]
        inter[2][p] = late[half:]
        return carry

    def hand_on(w, d, held):
        source = (z + NZ - d) % NZ
        tall = held.shape[1]

        def one(j, carry):
            yy, cc = member_of(j)
            entry = (z * MEMBERS + yy * NC + cc) * CAP
            outgoing[w][d, j, :tall] = held[picks[source, 0, 0, entry]]
            outgoing[w][d, j, tall:] = held[picks[source, 0, 0, entry + 1]]
            row_copy(w, d, j).start()
            return carry

        lax.fori_loop(1, MEMBERS, one, 0)
        entry = (z * MEMBERS + my_member) * CAP
        arrived[w][source, my_member, :tall] = held[picks[source, 0, 0, entry]]
        arrived[w][source, my_member, tall:] = held[picks[source, 0, 0, entry + 1]]

    def images(h, d):
        source = (z + NZ - d) % NZ

        def landed(j, carry):
            for w in HALVES[h]:
                row_copy(w, d, j).wait_recv()
            return carry

        lax.fori_loop(1, MEMBERS, landed, 0)

        def one(m, carry):
            made = []
            for r in range(CAP):
                tag = jnp.maximum(tags[m, source, 0, 0, (z * MEMBERS + my_member) * CAP + r], 0)
                lhs = jnp.concatenate(
                    [
                        left[t, tag, pl.ds(((x + dx) % NX) * rows, rows)]
                        for t in range(2)
                        for dx in range(NX)
                    ],
                    axis=0,
                )
                pieces = []
                for w in HALVES[h]:
                    tall = inter[w].shape[1]
                    pieces.append(arrived[w][source, m, r * tall : (r + 1) * tall])
                rhs = pieces[0] if len(pieces) == 1 else jnp.concatenate(pieces, axis=0)
                both = jnp.dot(lhs, rhs, preferred_element_type=jnp.float32)
                made.append((both[:width], both[width:]))
            pair = jnp.where(
                low, made[0][0] + turned(made[0][1]), turned(made[1][0]) + made[1][1]
            )
            at = source * MEMBERS + m
            own[h, at] = pair[:rows]
            for dx in range(1, NX):
                shares[h, dx - 1, at] = pair[dx * rows : (dx + 1) * rows].astype(shares.dtype)
            return carry

        lax.fori_loop(0, MEMBERS, one, 0, unroll=2)
        for dx in range(1, NX):
            term_copy(h, d, dx).start()

    plan = plan_of(owners[...], local[...], z)
    order_row[:, :count] = plan[0]
    to_order = pltpu.make_async_copy(order_row, order, local_sem.at[0])
    to_order.start()
    for k in range(3):
        table[k] = plan[k + 1]
    to_order.wait()
    loads[0].wait()
    loads[1].wait()
    edges = [0, *reversed(REACH)]
    spans = [
        [(edges[k], edges[k + 1]), (count - edges[k + 1], count - edges[k])] for k in range(HOPS)
    ]
    spans[-1] = [(edges[HOPS - 1], count - edges[HOPS - 1])]
    for k in range(HOPS):
        for begin, end in spans[k]:
            lax.fori_loop(begin, end, multiply, 0, unroll=True)
        if k == 0:
            pl.semaphore_wait(barrier, NZ - 1 + MEMBERS - 1 + NX - 1)
            for d in range(1, NZ):
                mate_copy(d).start()
        ring_copy(0, 0, 1, k).start()
        ring_copy(0, 1, 1, k).start()

    own_table = pltpu.make_async_copy(table, mates.at[z], local_sem.at[1])
    own_table.start()
    own_table.wait()
    for d in range(1, NZ):
        mate_copy(d).wait_recv()
    for j in range(1, MEMBERS):
        table_copy(j).start()
    to_picks = pltpu.make_async_copy(mates, picks, local_sem.at[2])
    to_picks.start()
    own_tables = pltpu.make_async_copy(mates, rowmates.at[my_member], local_sem.at[3])
    own_tables.start()
    to_picks.wait()
    for w in range(WAVES):
        hand_on(w, 0, inter[w])
    own_tables.wait()
    for j in range(1, MEMBERS):
        table_copy(j).wait_recv()
    to_tags = pltpu.make_async_copy(rowmates.at[:, :, pl.ds(1, 1)], tags, local_sem.at[4])
    to_tags.start()
    every = jnp.min(rowmates[:, :, 2, 0], axis=0)
    line_rows[4] = jnp.min(every, axis=0, keepdims=True)
    lane = lax.broadcasted_iota(jnp.int32, (1, 1, slots), 2)
    known = rowmates[:, :, 1, 0]
    mine = [
        jnp.sum(
            jnp.where(lane == (z * MEMBERS + my_member) * CAP + r, known, 0), axis=2, keepdims=True
        ).reshape(MEMBERS * NZ, 1)
        for r in range(CAP)
    ]
    row = lax.broadcasted_iota(jnp.int32, (slots, 1), 0)
    source_of, member_at = row % NZ, (row // NZ) % MEMBERS
    slot_at = source_of * per_source + member_at * CAP + row // (MEMBERS * NZ)
    line = sort_of(jnp.concatenate(mine, axis=0), slot_at)
    for k in range(4):
        line_rows[k] = line[k]
    to_lines = pltpu.make_async_copy(line_rows, lines, local_sem.at[5])
    to_lines.start()
    to_tags.wait()
    to_lines.wait()
    fit[0] = lines[4, 0, 0]
    loads[2].wait()

    early = {
        (0, 2, 0): [(0, 0), (1, 0)],
        (0, 3, 0): [(0, 1), (0, NZ - 1)],
        (1, 1, 0): [(0, 2), (0, NZ - 2)],
        (1, 2, 0): [(0, 3), (0, NZ - 3)],
        (1, 3, 0): [(0, 4)],
        (2, 2, 0): [(1, 1)],
        (2, 2, 1): [(1, NZ - 1)],
        (2, 3, 0): [(1, 2)],
        (2, 4, 0): [(1, NZ - 2)],
    }
    for w in range(WAVES):
        for hop in range(1, HOPS + 1):
            pieces = len(chunk_bounds(hop))
            for k in range(pieces):
                for way in range(2):
                    ring_copy(w, way, hop, k).wait_recv()
                if k < pieces - 1:
                    between = w < WAVES - 1 and hop == HOPS - 1
                    if between:
                        for late in range(HOPS - 1):
                            ring_copy(w + 1, 0, 1, late).start()
                            ring_copy(w + 1, 1, 1, late).start()
                    ring_copy(w, 0, hop + 1, k).start()
                    ring_copy(w, 1, hop + 1, k).start()
                    if between:
                        ring_copy(w + 1, 0, 1, HOPS - 1).start()
                        ring_copy(w + 1, 1, 1, HOPS - 1).start()
                    for h, d in early.get((w, hop, k), ()):
                        images(h, d)
            hand_on(w, hop, up[w][hop])
            if hop < HOPS:
                hand_on(w, NZ - hop, down[w][hop])
            for h, d in early.get((w, hop, pieces - 1), ()):
                images(h, d)
    for d in (HOPS - 1, NZ - HOPS + 1, HOPS):
        images(1, d)

    def settle(d):
        for h in range(2):
            for dx in range(1, NX):
                term_copy(h, d, dx).wait_recv()
        first = ((z + NZ - d) % NZ) * MEMBERS

        def add(i, carry):
            at = first + i
            left_half, right_half = (
                own[h, at]
                + (
                    taken[h, 0, at].astype(jnp.float32)
                    + taken[h, 1, at].astype(jnp.float32)
                    + taken[h, 2, at].astype(jnp.float32)
                )
                for h in range(2)
            )
            full[at * CAP] = jnp.where(low_rows, left_half, turned(right_half))
            full[at * CAP + 1] = jnp.where(low_rows, turned(left_half), right_half)
            return carry

        lax.fori_loop(0, MEMBERS, add, 0, unroll=4)

    for d in (0, 1, NZ - 1, 2, NZ - 2, HOPS - 1, NZ - HOPS + 1, HOPS):
        settle(d)

    def total(p, run):
        run = full[lines[0, 0, p]] + lines[1, 0, p].astype(jnp.float32) * run
        runs[p] = run
        return run

    lax.fori_loop(0, slots, total, jnp.zeros(full.shape[1:], jnp.float32), unroll=8)

    def give(l, carry):
        kept = lines[3, 0, l].astype(jnp.float32)
        out[l] = (kept * runs[lines[2, 0, l]]).astype(out.dtype)
        return carry

    lax.fori_loop(0, out.shape[0], give, 0, unroll=8)

    for w in range(WAVES):
        for way in range(2):
            for hop, k in number:
                ring_copy(w, way, hop, k).wait_send()
    for d in range(1, NZ):
        mate_copy(d).wait_send()
    for j in range(1, MEMBERS):
        table_copy(j).wait_send()

    def sent(d, carry):
        for j in range(1, MEMBERS):
            for w in range(WAVES):
                row_copy(w, d, j).wait_send()
        for h in range(2):
            for dx in range(1, NX):
                term_copy(h, d, dx).wait_send()
        return carry

    lax.fori_loop(0, NZ, sent, 0)


def image_kernel(tags_ref, left_ref, arrived_ref, out_ref, acc):
    slots = arrived_ref.shape[0]
    acc[...] = jnp.zeros_like(acc)

    def step(i, carry):
        tag = tags_ref[i]

        @pl.when(tag >= 0)
        def _():
            lhs = jnp.concatenate([left_ref[0, tag], left_ref[1, tag]], axis=-1)
            acc[tag] += jnp.dot(lhs, arrived_ref[i], preferred_element_type=jnp.float32)

        return carry

    lax.fori_loop(0, slots, step, 0)
    out_ref[...] = acc[...]


SMEM = pl.BlockSpec(memory_space=pltpu.SMEM)
VMEM = pl.BlockSpec(memory_space=pltpu.VMEM)
ANY = pl.BlockSpec(memory_space=pl.ANY)


def full_exchange(psi_blocks, right_ops, slot_source, left_ops, tags):
    terms, sec_dev, width, _ = left_ops.shape
    inter = (
        jnp.einsum("sij,tsjk->stik", psi_blocks, right_ops, preferred_element_type=jnp.float32)
        .astype(jnp.bfloat16)
        .reshape(sec_dev, terms * width, width)
    )
    packed = jnp.take(inter, slot_source, axis=0, mode="clip")
    arrived = lax.all_to_all(packed, "sector", split_axis=0, concat_axis=0, tiled=True)
    partial = pl.pallas_call(
        image_kernel,
        out_shape=jax.ShapeDtypeStruct((sec_dev, width, width), jnp.float32),
        in_specs=[SMEM, VMEM, VMEM],
        out_specs=VMEM,
        scratch_shapes=[pltpu.VMEM((sec_dev, width, width), jnp.float32)],
        compiler_params=pltpu.CompilerParams(vmem_limit_bytes=48 << 20),
        name="images",
    )(tags, left_ops, arrived)
    parts = lax.all_to_all(
        partial.reshape(sec_dev, NX, width // NX, width), "term", split_axis=1, concat_axis=1
    )
    return jnp.sum(parts, axis=1).astype(jnp.bfloat16)


def ring_exchange(owners, local, psi_blocks, right_ops, left_ops):
    terms, sec_dev, width, _ = left_ops.shape
    slots = NZ * MEMBERS * CAP
    rows = width // NX
    dma = pltpu.SemaphoreType.DMA
    pieces = sum(range(1, HOPS + 1))

    def blocks(*lead, tall=width):
        return pltpu.VMEM((*lead, tall, width), jnp.bfloat16)

    talls = (width, width // 2, width // 2)
    inter = [blocks(sec_dev, tall=t) for t in talls]
    waves = []
    for t in talls:
        waves += [blocks(REACH[h], tall=t) for h in (0, 1, 2)] * 2 + [blocks(2 * REACH[3], tall=t)]
    row_blocks = [blocks(NZ, MEMBERS, tall=CAP * t) for t in talls]
    return pl.pallas_call(
        ring_kernel,
        out_shape=(
            jax.ShapeDtypeStruct((sec_dev, rows, width), jnp.bfloat16),
            jax.ShapeDtypeStruct((1,), jnp.int32),
        ),
        in_specs=[VMEM, VMEM, ANY, ANY, ANY],
        out_specs=(VMEM, SMEM),
        scratch_shapes=[
            blocks(sec_dev),
            blocks(terms, sec_dev),
            blocks(terms, sec_dev),
            *inter,
            *waves,
            *row_blocks,
            *row_blocks,
            pltpu.VMEM((2, NX - 1, slots // CAP, rows, width), jnp.bfloat16),
            pltpu.VMEM((2, NX - 1, slots // CAP, rows, width), jnp.bfloat16),
            pltpu.VMEM((2, slots // CAP, rows, width), jnp.float32),
            pltpu.VMEM((slots, rows, width), jnp.float32),
            pltpu.VMEM((slots, rows, width), jnp.float32),
            pltpu.VMEM((1, slots), jnp.int32),
            pltpu.SMEM((1, slots), jnp.int32),
            pltpu.VMEM((3, 1, slots), jnp.int32),
            pltpu.VMEM((NZ, 3, 1, slots), jnp.int32),
            pltpu.SMEM((NZ, 3, 1, slots), jnp.int32),
            pltpu.VMEM((MEMBERS, NZ, 3, 1, slots), jnp.int32),
            pltpu.SMEM((MEMBERS, NZ, 1, 1, slots), jnp.int32),
            pltpu.VMEM((5, 1, slots), jnp.int32),
            pltpu.SMEM((5, 1, slots), jnp.int32),
            dma((3,)),
            dma((6,)),
            dma((WAVES, 2, pieces)),
            dma((WAVES, 2, pieces)),
            dma((WAVES, NZ, MEMBERS)),
            dma((WAVES, NZ, MEMBERS)),
            dma((2, NZ, NX)),
            dma((2, NZ, NX)),
            dma((NZ,)),
            dma((NZ,)),
            dma((MEMBERS,)),
            dma((MEMBERS,)),
        ],
        compiler_params=pltpu.CompilerParams(
            collective_id=0, has_side_effects=True, vmem_limit_bytes=63 << 20
        ),
        name="ring",
    )(owners, local, psi_blocks, right_ops, left_ops)


def local(psi_blocks, right_ops, left_ops, owner_map, left_local):
    sec_dev, width, _ = psi_blocks.shape
    n_sector = lax.axis_size("sector")
    slots = n_sector * CAP
    found, fit = ring_exchange(
        owner_map.reshape(1, sec_dev), left_local.reshape(1, sec_dev), psi_blocks, right_ops, left_ops
    )

    def by_ring(found, psi_blocks, right_ops, left_ops, owner_map, left_local):
        return found

    def by_all(found, psi_blocks, right_ops, left_ops, owner_map, left_local):
        owners = owner_map[:, 0]
        slot_id = owners * CAP + ranks_of(owners)
        hot = slot_id[None, :] == lax.broadcasted_iota(jnp.int32, (slots, sec_dev), 0)
        slot_source = jnp.sum(
            jnp.where(hot, lax.broadcasted_iota(jnp.int32, (slots, sec_dev), 1), 0), axis=1
        )
        own_tags = jnp.max(jnp.where(hot, left_local[:, 0][None, :], -1), axis=1)
        tags = lax.all_to_all(
            own_tags.reshape(n_sector, CAP), "sector", split_axis=0, concat_axis=0, tiled=True
        ).reshape(slots)
        return full_exchange(psi_blocks, right_ops, slot_source, left_ops, tags)

    return lax.cond(
        fit[0] > 0, by_ring, by_all, found, psi_blocks, right_ops, left_ops, owner_map, left_local
    )


def solution(mesh):
    placed = (
        P("sector", None, None),
        P("term", "sector", None, None),
        P("term", "sector", None, None),
        P("sector", None),
        P("sector", None),
    )
    return jax.shard_map(
        local, mesh=mesh, in_specs=placed, out_specs=P("sector", "term", None), check_vma=False
    )
```

```python
import functools

import jax
import jax.numpy as jnp
from jax import lax
from jax.experimental import pallas as pl
from jax.experimental.pallas import tpu as pltpu
from jax.sharding import PartitionSpec as P

MESH = pl.DeviceIdType.MESH
CAP = 2
NY, NZ, NC = 4, 8, 2
NX = 4
MEMBERS = NY * NC
REACH = (33, 24, 16, 7)
HOPS = len(REACH)
WAVES = 3
HALVES = ((0,), (1, 2))


def chunk_bounds(hop):
    edges = [0, *reversed(REACH[hop - 1 :])]
    return list(zip(edges[:-1], edges[1:]))


def ranks_of(owners):
    count = owners.shape[-1]
    same = owners[..., :, None] == owners[..., None, :]
    earlier = lax.broadcasted_iota(jnp.int32, (count, count), 0) < lax.broadcasted_iota(
        jnp.int32, (count, count), 1
    )
    return jnp.sum((same & earlier).astype(jnp.int32), axis=-2)


def down_of(row):
    n = row.shape[1]
    same = lax.broadcasted_iota(jnp.int32, (n, n), 0) == lax.broadcasted_iota(jnp.int32, (n, n), 1)
    return jnp.sum(jnp.where(same, row, 0), axis=1, keepdims=True)


def across_of(column):
    n = column.shape[0]
    same = lax.broadcasted_iota(jnp.int32, (n, n), 0) == lax.broadcasted_iota(jnp.int32, (n, n), 1)
    return jnp.sum(jnp.where(same, column, 0), axis=0, keepdims=True)


def count_down(hits):
    return jnp.sum(jnp.where(hits, 1, 0), axis=0, keepdims=True)


def count_across(hits):
    return jnp.sum(jnp.where(hits, 1, 0), axis=1, keepdims=True)


def plan_of(owners, local, z):
    n = owners.shape[1]
    i = lax.broadcasted_iota(jnp.int32, (n, n), 0)
    j = lax.broadcasted_iota(jnp.int32, (n, n), 1)
    owners_down = down_of(owners)
    ranks = count_down((owners_down == owners) & (i < j))
    away = ((owners // NC) % NZ - z + NZ) % NZ
    counts = [count_across(away == d) for d in range(NZ)]
    up = [sum(counts[h:HOPS]) for h in range(1, HOPS)] + [0]
    down = [sum(counts[NZ - h] for h in range(k, HOPS)) for k in range(1, HOPS)] + [0]
    room_up = functools.reduce(jnp.minimum, [REACH[h] - up[h] for h in range(HOPS)])
    room_down = functools.reduce(jnp.minimum, [REACH[h] - down[h] for h in range(HOPS)])
    far_up = jnp.minimum(jnp.maximum(room_up, 0), counts[HOPS])
    fits = jnp.where((room_up >= 0) & (room_down >= counts[HOPS] - far_up), 1, 0)
    opposite = down_of(jnp.where(away == HOPS, 1, 0))
    far_rank = jnp.sum(jnp.where(i < j, opposite, 0), axis=0, keepdims=True)
    signed = jnp.where(
        away == HOPS,
        jnp.where(far_rank < far_up, -HOPS, HOPS),
        jnp.where(away < HOPS, -away, NZ - away),
    )
    key = signed * n + j[:1]
    position = count_down(down_of(key) < key)
    position_down = down_of(position)
    order = jnp.sum(jnp.where(position_down == j, i, 0), axis=0, keepdims=True)

    wide = NZ * MEMBERS * CAP
    entry = lax.broadcasted_iota(jnp.int32, (1, wide), 1)
    mate = entry // (MEMBERS * CAP)
    member = (entry // CAP) % MEMBERS
    goal = ((member // NC) * NZ + mate) * NC + member % NC
    hits = (owners_down == goal) & (down_of(ranks) == entry % CAP)
    ahead = (mate - z + NZ) % NZ
    start, size = jnp.zeros_like(ahead), jnp.full_like(ahead, n)
    for h in range(1, HOPS):
        start = jnp.where(ahead == NZ - h, n - REACH[h - 1], start)
        size = jnp.where((ahead == h) | (ahead == NZ - h), REACH[h - 1], size)
    size = jnp.where(ahead == HOPS, 2 * REACH[-1], size)
    where = jnp.sum(jnp.where(hits, position_down, 0), axis=0, keepdims=True) - start
    where = jnp.where((ahead == HOPS) & (where >= REACH[-1]), where - (n - 2 * REACH[-1]), where)
    where = jnp.minimum(jnp.maximum(where, 0), size - 1)
    tags = jnp.sum(jnp.where(hits, down_of(local) + 1, 0), axis=0, keepdims=True) - 1
    return order, where, tags, jnp.broadcast_to(fits, (1, wide))


def sort_of(tags, slots):
    n = tags.shape[0]
    place = lax.broadcasted_iota(jnp.int32, (n, n), 1)
    tags = jnp.where(tags < 0, n // CAP, tags)
    key = tags * n + lax.broadcasted_iota(jnp.int32, (n, 1), 0)
    earlier = across_of(key) < key
    at = count_across(earlier)
    follows = jnp.where(count_across(earlier & (across_of(tags) == tags)) > 0, 1, 0)
    order = jnp.sum(jnp.where(at == place, slots, 0), axis=0, keepdims=True)
    keep = jnp.sum(jnp.where(at == place, follows, 0), axis=0, keepdims=True)
    last = jnp.maximum(count_down(tags <= place) - 1, 0)
    has = jnp.where(count_down(tags == place) > 0, 1, 0)
    return order, keep, last, has


def ring_kernel(owners, local, psi_far, right_far, left_far, out, fit, psi, right, left, *refs):
    refs = list(refs)

    def take(number):
        taken_refs = refs[:number]
        del refs[:number]
        return taken_refs

    inter = take(WAVES)
    up, down = [], []
    for w in range(WAVES):
        up1, up2, up3, down1, down2, down3, far = take(7)
        up.append((inter[w], up1, up2, up3, far))
        down.append((inter[w], down1, down2, down3, far))
    outgoing, arrived = take(WAVES), take(WAVES)
    shares, taken, own, full, runs = take(5)
    order_row, order, table, mates, picks, rowmates, tags, line_rows, lines = take(9)
    load, local_sem, ring_send, ring_recv, row_send, row_recv, term_send, term_recv = take(8)
    mate_send, mate_recv, table_send, table_recv = take(4)
    count, width = psi.shape[0], psi.shape[1]
    rows = out.shape[1]
    slots = full.shape[0]
    half = width // 2
    per_source = MEMBERS * CAP
    x = lax.axis_index("term")
    place = lax.axis_index("sector")
    c = place % NC
    z = (place // NC) % NZ
    y = place // (NC * NZ)
    my_member = y * NC + c

    def sector_id(yy, zz, cc):
        return {"sector": (yy * NZ + zz) * NC + cc}

    def member_of(j):
        return (y + j // NC) % NY, (c + j) % NC

    z_up, z_down = (z + 1) % NZ, (z + NZ - 1) % NZ
    loads = [
        pltpu.make_async_copy(psi_far, psi, load.at[0]),
        pltpu.make_async_copy(right_far, right, load.at[1]),
        pltpu.make_async_copy(left_far, left, load.at[2]),
    ]
    for copy in loads:
        copy.start()
    barrier = pltpu.get_barrier_semaphore()
    for d in range(1, NZ):
        pl.semaphore_signal(
            barrier, inc=1, device_id=sector_id(y, (z + d) % NZ, c), device_id_type=MESH
        )
    for j in range(1, MEMBERS):
        yy, cc = member_of(j)
        pl.semaphore_signal(barrier, inc=1, device_id=sector_id(yy, z, cc), device_id_type=MESH)
    for d in range(1, NX):
        pl.semaphore_signal(barrier, inc=1, device_id={"term": (x + d) % NX}, device_id_type=MESH)

    reach_far = REACH[-1]
    number = {}
    for hop in range(1, HOPS + 1):
        for k in range(len(chunk_bounds(hop))):
            number[hop, k] = len(number)

    def ring_copy(w, way, hop, k):
        near, end = chunk_bounds(hop)[k]
        size = end - near
        if way == 0:
            source, target, neighbour = up[w][hop - 1], up[w][hop], z_up
            src_at, dst_at = near, near
        else:
            source, target, neighbour = down[w][hop - 1], down[w][hop], z_down
            held = count if hop == 1 else REACH[hop - 2]
            src_at = held - end
            dst_at = REACH[hop - 1] - end + (reach_far if hop == HOPS else 0)
        return pltpu.make_async_remote_copy(
            src_ref=source.at[pl.ds(src_at, size)],
            dst_ref=target.at[pl.ds(dst_at, size)],
            send_sem=ring_send.at[w, way, number[hop, k]],
            recv_sem=ring_recv.at[w, way, number[hop, k]],
            device_id=sector_id(y, neighbour, c),
            device_id_type=MESH,
        )

    def row_copy(w, d, j):
        yy, cc = member_of(j)
        return pltpu.make_async_remote_copy(
            src_ref=outgoing[w].at[d, j],
            dst_ref=arrived[w].at[(z + NZ - d) % NZ, my_member],
            send_sem=row_send.at[w, d, j],
            recv_sem=row_recv.at[w, d, j],
            device_id=sector_id(yy, z, cc),
            device_id_type=MESH,
        )

    def term_copy(h, d, dx):
        group = pl.ds(((z + NZ - d) % NZ) * MEMBERS, MEMBERS)
        return pltpu.make_async_remote_copy(
            src_ref=shares.at[h, dx - 1, group],
            dst_ref=taken.at[h, dx - 1, group],
            send_sem=term_send.at[h, d, dx],
            recv_sem=term_recv.at[h, d, dx],
            device_id={"term": (x + dx) % NX},
            device_id_type=MESH,
        )

    def mate_copy(d):
        mate = (z + d) % NZ
        return pltpu.make_async_remote_copy(
            src_ref=table,
            dst_ref=mates.at[z],
            send_sem=mate_send.at[d],
            recv_sem=mate_recv.at[d],
            device_id=sector_id(y, mate, c),
            device_id_type=MESH,
        )

    def table_copy(j):
        yy, cc = member_of(j)
        return pltpu.make_async_remote_copy(
            src_ref=mates,
            dst_ref=rowmates.at[my_member],
            send_sem=table_send.at[j],
            recv_sem=table_recv.at[j],
            device_id=sector_id(yy, z, cc),
            device_id_type=MESH,
        )

    low = lax.broadcasted_iota(jnp.int32, (width, width), 1) < half
    low_rows = lax.broadcasted_iota(jnp.int32, (rows, width), 1) < half

    def turned(value):
        return pltpu.roll(value, half, 1)

    def multiply(p, carry):
        s = order[0, p]
        both = jnp.concatenate([right[0, s], right[1, s]], axis=-1)
        made = jnp.dot(psi[s], both, preferred_element_type=jnp.float32)
        one, two = made[:, :width], made[:, width:]
        inter[0][p] = jnp.where(low, one, turned(two)).astype(jnp.bfloat16)
        late = jnp.where(low, turned(one), two).astype(jnp.bfloat16)
        inter[1][p] = late[:half]
        inter[2][p] = late[half:]
        return carry

    def hand_on(w, d, held):
        source = (z + NZ - d) % NZ
        tall = held.shape[1]

        def one(j, carry):
            yy, cc = member_of(j)
            entry = (z * MEMBERS + yy * NC + cc) * CAP
            outgoing[w][d, j, :tall] = held[picks[source, 0, 0, entry]]
            outgoing[w][d, j, tall:] = held[picks[source, 0, 0, entry + 1]]
            row_copy(w, d, j).start()
            return carry

        lax.fori_loop(1, MEMBERS, one, 0)
        entry = (z * MEMBERS + my_member) * CAP
        arrived[w][source, my_member, :tall] = held[picks[source, 0, 0, entry]]
        arrived[w][source, my_member, tall:] = held[picks[source, 0, 0, entry + 1]]

    def images(h, d):
        source = (z + NZ - d) % NZ

        def landed(j, carry):
            for w in HALVES[h]:
                row_copy(w, d, j).wait_recv()
            return carry

        lax.fori_loop(1, MEMBERS, landed, 0)

        def one(m, carry):
            made = []
            for r in range(CAP):
                tag = jnp.maximum(tags[m, source, 0, 0, (z * MEMBERS + my_member) * CAP + r], 0)
                lhs = jnp.concatenate(
                    [
                        left[t, tag, pl.ds(((x + dx) % NX) * rows, rows)]
                        for t in range(2)
                        for dx in range(NX)
                    ],
                    axis=0,
                )
                pieces = []
                for w in HALVES[h]:
                    tall = inter[w].shape[1]
                    pieces.append(arrived[w][source, m, r * tall : (r + 1) * tall])
                rhs = pieces[0] if len(pieces) == 1 else jnp.concatenate(pieces, axis=0)
                both = jnp.dot(lhs, rhs, preferred_element_type=jnp.float32)
                made.append((both[:width], both[width:]))
            pair = jnp.where(
                low, made[0][0] + turned(made[0][1]), turned(made[1][0]) + made[1][1]
            )
            at = source * MEMBERS + m
            own[h, at] = pair[:rows]
            for dx in range(1, NX):
                shares[h, dx - 1, at] = pair[dx * rows : (dx + 1) * rows].astype(shares.dtype)
            return carry

        lax.fori_loop(0, MEMBERS, one, 0, unroll=2)
        for dx in range(1, NX):
            term_copy(h, d, dx).start()

    plan = plan_of(owners[...], local[...], z)
    order_row[:, :count] = plan[0]
    to_order = pltpu.make_async_copy(order_row, order, local_sem.at[0])
    to_order.start()
    for k in range(3):
        table[k] = plan[k + 1]
    to_order.wait()
    loads[0].wait()
    loads[1].wait()
    edges = [0, *reversed(REACH)]
    spans = [
        [(edges[k], edges[k + 1]), (count - edges[k + 1], count - edges[k])] for k in range(HOPS)
    ]
    spans[-1] = [(edges[HOPS - 1], count - edges[HOPS - 1])]
    for k in range(HOPS):
        for begin, end in spans[k]:
            lax.fori_loop(begin, end, multiply, 0, unroll=True)
        if k == 0:
            pl.semaphore_wait(barrier, NZ - 1 + MEMBERS - 1 + NX - 1)
            for d in range(1, NZ):
                mate_copy(d).start()
        ring_copy(0, 0, 1, k).start()
        ring_copy(0, 1, 1, k).start()

    own_table = pltpu.make_async_copy(table, mates.at[z], local_sem.at[1])
    own_table.start()
    own_table.wait()
    for d in range(1, NZ):
        mate_copy(d).wait_recv()
    for j in range(1, MEMBERS):
        table_copy(j).start()
    to_picks = pltpu.make_async_copy(mates, picks, local_sem.at[2])
    to_picks.start()
    own_tables = pltpu.make_async_copy(mates, rowmates.at[my_member], local_sem.at[3])
    own_tables.start()
    to_picks.wait()
    for w in range(WAVES):
        hand_on(w, 0, inter[w])
    own_tables.wait()
    for j in range(1, MEMBERS):
        table_copy(j).wait_recv()
    to_tags = pltpu.make_async_copy(rowmates.at[:, :, pl.ds(1, 1)], tags, local_sem.at[4])
    to_tags.start()
    every = jnp.min(rowmates[:, :, 2, 0], axis=0)
    line_rows[4] = jnp.min(every, axis=0, keepdims=True)
    lane = lax.broadcasted_iota(jnp.int32, (1, 1, slots), 2)
    known = rowmates[:, :, 1, 0]
    mine = [
        jnp.sum(
            jnp.where(lane == (z * MEMBERS + my_member) * CAP + r, known, 0), axis=2, keepdims=True
        ).reshape(MEMBERS * NZ, 1)
        for r in range(CAP)
    ]
    row = lax.broadcasted_iota(jnp.int32, (slots, 1), 0)
    source_of, member_at = row % NZ, (row // NZ) % MEMBERS
    slot_at = source_of * per_source + member_at * CAP + row // (MEMBERS * NZ)
    line = sort_of(jnp.concatenate(mine, axis=0), slot_at)
    for k in range(4):
        line_rows[k] = line[k]
    to_lines = pltpu.make_async_copy(line_rows, lines, local_sem.at[5])
    to_lines.start()
    to_tags.wait()
    to_lines.wait()
    fit[0] = lines[4, 0, 0]
    loads[2].wait()

    early = {
        (0, 2, 0): [(0, 0), (1, 0)],
        (0, 3, 0): [(0, 1), (0, NZ - 1)],
        (1, 1, 0): [(0, 2), (0, NZ - 2)],
        (1, 2, 0): [(0, 3), (0, NZ - 3)],
        (1, 3, 0): [(0, 4)],
        (2, 2, 0): [(1, 1)],
        (2, 2, 1): [(1, NZ - 1)],
        (2, 3, 0): [(1, 2)],
        (2, 3, 1): [(1, NZ - 2)],
    }
    for w in range(WAVES):
        for hop in range(1, HOPS + 1):
            pieces = len(chunk_bounds(hop))
            for k in range(pieces):
                for way in range(2):
                    ring_copy(w, way, hop, k).wait_recv()
                if k < pieces - 1:
                    between = w < WAVES - 1 and hop == HOPS - 1
                    if between:
                        for late in range(HOPS - 1):
                            ring_copy(w + 1, 0, 1, late).start()
                            ring_copy(w + 1, 1, 1, late).start()
                    ring_copy(w, 0, hop + 1, k).start()
                    ring_copy(w, 1, hop + 1, k).start()
                    if between:
                        ring_copy(w + 1, 0, 1, HOPS - 1).start()
                        ring_copy(w + 1, 1, 1, HOPS - 1).start()
                    for h, d in early.get((w, hop, k), ()):
                        images(h, d)
            hand_on(w, hop, up[w][hop])
            if hop < HOPS:
                hand_on(w, NZ - hop, down[w][hop])
            for h, d in early.get((w, hop, pieces - 1), ()):
                images(h, d)
    for d in (HOPS - 1, NZ - HOPS + 1, HOPS):
        images(1, d)

    def settle(d):
        for h in range(2):
            for dx in range(1, NX):
                term_copy(h, d, dx).wait_recv()
        first = ((z + NZ - d) % NZ) * MEMBERS

        def add(i, carry):
            at = first + i
            left_half, right_half = (
                own[h, at]
                + (
                    taken[h, 0, at].astype(jnp.float32)
                    + taken[h, 1, at].astype(jnp.float32)
                    + taken[h, 2, at].astype(jnp.float32)
                )
                for h in range(2)
            )
            full[at * CAP] = jnp.where(low_rows, left_half, turned(right_half))
            full[at * CAP + 1] = jnp.where(low_rows, turned(left_half), right_half)
            return carry

        lax.fori_loop(0, MEMBERS, add, 0, unroll=4)

    for d in (0, 1, NZ - 1, 2, NZ - 2, HOPS - 1, NZ - HOPS + 1, HOPS):
        settle(d)

    def total(p, run):
        run = full[lines[0, 0, p]] + lines[1, 0, p].astype(jnp.float32) * run
        runs[p] = run
        return run

    lax.fori_loop(0, slots, total, jnp.zeros(full.shape[1:], jnp.float32), unroll=8)

    def give(l, carry):
        kept = lines[3, 0, l].astype(jnp.float32)
        out[l] = (kept * runs[lines[2, 0, l]]).astype(out.dtype)
        return carry

    lax.fori_loop(0, out.shape[0], give, 0, unroll=8)

    for w in range(WAVES):
        for way in range(2):
            for hop, k in number:
                ring_copy(w, way, hop, k).wait_send()
    for d in range(1, NZ):
        mate_copy(d).wait_send()
    for j in range(1, MEMBERS):
        table_copy(j).wait_send()

    def sent(d, carry):
        for j in range(1, MEMBERS):
            for w in range(WAVES):
                row_copy(w, d, j).wait_send()
        for h in range(2):
            for dx in range(1, NX):
                term_copy(h, d, dx).wait_send()
        return carry

    lax.fori_loop(0, NZ, sent, 0)


def image_kernel(tags_ref, left_ref, arrived_ref, out_ref, acc):
    slots = arrived_ref.shape[0]
    acc[...] = jnp.zeros_like(acc)

    def step(i, carry):
        tag = tags_ref[i]

        @pl.when(tag >= 0)
        def _():
            lhs = jnp.concatenate([left_ref[0, tag], left_ref[1, tag]], axis=-1)
            acc[tag] += jnp.dot(lhs, arrived_ref[i], preferred_element_type=jnp.float32)

        return carry

    lax.fori_loop(0, slots, step, 0)
    out_ref[...] = acc[...]


SMEM = pl.BlockSpec(memory_space=pltpu.SMEM)
VMEM = pl.BlockSpec(memory_space=pltpu.VMEM)
ANY = pl.BlockSpec(memory_space=pl.ANY)


def full_exchange(psi_blocks, right_ops, slot_source, left_ops, tags):
    terms, sec_dev, width, _ = left_ops.shape
    inter = (
        jnp.einsum("sij,tsjk->stik", psi_blocks, right_ops, preferred_element_type=jnp.float32)
        .astype(jnp.bfloat16)
        .reshape(sec_dev, terms * width, width)
    )
    packed = jnp.take(inter, slot_source, axis=0, mode="clip")
    arrived = lax.all_to_all(packed, "sector", split_axis=0, concat_axis=0, tiled=True)
    partial = pl.pallas_call(
        image_kernel,
        out_shape=jax.ShapeDtypeStruct((sec_dev, width, width), jnp.float32),
        in_specs=[SMEM, VMEM, VMEM],
        out_specs=VMEM,
        scratch_shapes=[pltpu.VMEM((sec_dev, width, width), jnp.float32)],
        compiler_params=pltpu.CompilerParams(vmem_limit_bytes=48 << 20),
        name="images",
    )(tags, left_ops, arrived)
    parts = lax.all_to_all(
        partial.reshape(sec_dev, NX, width // NX, width), "term", split_axis=1, concat_axis=1
    )
    return jnp.sum(parts, axis=1).astype(jnp.bfloat16)


def ring_exchange(owners, local, psi_blocks, right_ops, left_ops):
    terms, sec_dev, width, _ = left_ops.shape
    slots = NZ * MEMBERS * CAP
    rows = width // NX
    dma = pltpu.SemaphoreType.DMA
    pieces = sum(range(1, HOPS + 1))

    def blocks(*lead, tall=width):
        return pltpu.VMEM((*lead, tall, width), jnp.bfloat16)

    talls = (width, width // 2, width // 2)
    inter = [blocks(sec_dev, tall=t) for t in talls]
    waves = []
    for t in talls:
        waves += [blocks(REACH[h], tall=t) for h in (0, 1, 2)] * 2 + [blocks(2 * REACH[3], tall=t)]
    row_blocks = [blocks(NZ, MEMBERS, tall=CAP * t) for t in talls]
    return pl.pallas_call(
        ring_kernel,
        out_shape=(
            jax.ShapeDtypeStruct((sec_dev, rows, width), jnp.bfloat16),
            jax.ShapeDtypeStruct((1,), jnp.int32),
        ),
        in_specs=[VMEM, VMEM, ANY, ANY, ANY],
        out_specs=(VMEM, SMEM),
        scratch_shapes=[
            blocks(sec_dev),
            blocks(terms, sec_dev),
            blocks(terms, sec_dev),
            *inter,
            *waves,
            *row_blocks,
            *row_blocks,
            pltpu.VMEM((2, NX - 1, slots // CAP, rows, width), jnp.bfloat16),
            pltpu.VMEM((2, NX - 1, slots // CAP, rows, width), jnp.bfloat16),
            pltpu.VMEM((2, slots // CAP, rows, width), jnp.float32),
            pltpu.VMEM((slots, rows, width), jnp.float32),
            pltpu.VMEM((slots, rows, width), jnp.float32),
            pltpu.VMEM((1, slots), jnp.int32),
            pltpu.SMEM((1, slots), jnp.int32),
            pltpu.VMEM((3, 1, slots), jnp.int32),
            pltpu.VMEM((NZ, 3, 1, slots), jnp.int32),
            pltpu.SMEM((NZ, 3, 1, slots), jnp.int32),
            pltpu.VMEM((MEMBERS, NZ, 3, 1, slots), jnp.int32),
            pltpu.SMEM((MEMBERS, NZ, 1, 1, slots), jnp.int32),
            pltpu.VMEM((5, 1, slots), jnp.int32),
            pltpu.SMEM((5, 1, slots), jnp.int32),
            dma((3,)),
            dma((6,)),
            dma((WAVES, 2, pieces)),
            dma((WAVES, 2, pieces)),
            dma((WAVES, NZ, MEMBERS)),
            dma((WAVES, NZ, MEMBERS)),
            dma((2, NZ, NX)),
            dma((2, NZ, NX)),
            dma((NZ,)),
            dma((NZ,)),
            dma((MEMBERS,)),
            dma((MEMBERS,)),
        ],
        compiler_params=pltpu.CompilerParams(
            collective_id=0, has_side_effects=True, vmem_limit_bytes=63 << 20
        ),
        name="ring",
    )(owners, local, psi_blocks, right_ops, left_ops)


def local(psi_blocks, right_ops, left_ops, owner_map, left_local):
    sec_dev, width, _ = psi_blocks.shape
    n_sector = lax.axis_size("sector")
    slots = n_sector * CAP
    found, fit = ring_exchange(
        owner_map.reshape(1, sec_dev), left_local.reshape(1, sec_dev), psi_blocks, right_ops, left_ops
    )

    def by_ring(found, psi_blocks, right_ops, left_ops, owner_map, left_local):
        return found

    def by_all(found, psi_blocks, right_ops, left_ops, owner_map, left_local):
        owners = owner_map[:, 0]
        slot_id = owners * CAP + ranks_of(owners)
        hot = slot_id[None, :] == lax.broadcasted_iota(jnp.int32, (slots, sec_dev), 0)
        slot_source = jnp.sum(
            jnp.where(hot, lax.broadcasted_iota(jnp.int32, (slots, sec_dev), 1), 0), axis=1
        )
        own_tags = jnp.max(jnp.where(hot, left_local[:, 0][None, :], -1), axis=1)
        tags = lax.all_to_all(
            own_tags.reshape(n_sector, CAP), "sector", split_axis=0, concat_axis=0, tiled=True
        ).reshape(slots)
        return full_exchange(psi_blocks, right_ops, slot_source, left_ops, tags)

    return lax.cond(
        fit[0] > 0, by_ring, by_all, found, psi_blocks, right_ops, left_ops, owner_map, left_local
    )


def solution(mesh):
    placed = (
        P("sector", None, None),
        P("term", "sector", None, None),
        P("term", "sector", None, None),
        P("sector", None),
        P("sector", None),
    )
    return jax.shard_map(
        local, mesh=mesh, in_specs=placed, out_specs=P("sector", "term", None), check_vma=False
    )
```
